512 devices in a mesh: ctx: 64 (over y_lo, z, core), head: 8 (over y_hi, x).
Axes of the slice: x: 4, y: 4 (y_hi: 2, y_lo: 2; y = y_hi * 2 + y_lo), z: 16, core: 2. Of those that a mesh axis runs over, the one named last changes fastest.
Arguments:
- queries: bfloat16 [8192, 2048], P('ctx', 'head'), may hold values from -8 to 8, as said below
- key_codes: bfloat16 [2, 8192, 128], P(None, 'ctx'), may hold values from -6 to 6
- key_scale: float32 [2, 8192], P(None, 'ctx'), may hold values from 0.5 to 2
- value_codes: bfloat16 [2, 8192, 128], P(None, 'ctx'), may hold values from -6 to 6
- value_scale: float32 [2, 8192], P(None, 'ctx'), may hold values from 0.5 to 2
- evict_flags: int32 [2, 8192], P(None, 'ctx'), may hold values from 0 to 1, as said below
- out_forward: bfloat16 [8192, 2048], P('ctx', 'head'), may hold values from -12 to 12, as said below
- grad_output: bfloat16 [8192, 2048], P('ctx', 'head'), may hold values from -6 to 6
- log_norm: float32 [16, 8192], P('head', 'ctx'), as said below
Outputs:
- grad_queries: bfloat16 [8192, 2048], P('ctx', 'head')
- grad_keys: bfloat16 [2, 8192, 128], P(None, 'ctx')
- grad_values: bfloat16 [2, 8192, 128], P(None, 'ctx')
The draws below stay inside these ranges and needn't reach their ends.
Inputs may be any that keep to these rules, and one draw needn't show every extreme that they name: queries hold bfloat16 values. `evict_flags`: each token and key and value head is evicted independently with probability one half. log_norm is the log of the sum of exp(c * scores) over the visible keys of each query, from the same queries, keys and flags. out_forward is the forward attention output of the same inputs, rounded to bfloat16.
All inputs are finite; a program needn't handle non-finite values.
Results may differ from the reference program's by a relative error of at most 0.0033.
The reference program's roundings to bfloat16 on the way count: a program that leaves them out, or rounds other values in their place, can miss the bound.
Values may be sent and summed in bfloat16 or wider, within the bound.
No kernel may reach another device: no remote copies, remote signals or barrier semaphores. Data moves between devices by JAX's collectives and lax.ppermute only.
A program may use at most 64 MiB of HBM per device.

```python
import math
import jax
import jax.numpy as jnp
from jax import lax

CHANNEL_DIM = 128
ASKER_PROJ_NUM = 16
KEY_VALUE_HEADS = 2
TOK_DEV = 128
SEQUENCE_TOKENS = 8192
DELAY = 256


def token_position_drawn(rows, tok_dev, ctx_count):
    device_row = rows // tok_dev
    within = rows % tok_dev
    half = tok_dev // 2
    return jnp.where(within < half, device_row * half + within, (2 * ctx_count - 1 - device_row) * half + within - half).astype(jnp.int32)


def base_inputs(key):
    queries = jax.random.normal(jax.random.fold_in(key, 101), (SEQUENCE_TOKENS, ASKER_PROJ_NUM * CHANNEL_DIM), jnp.float32)
    value_codes = jnp.clip(jax.random.normal(jax.random.fold_in(key, 103), (KEY_VALUE_HEADS, SEQUENCE_TOKENS, CHANNEL_DIM), jnp.float32), -6.0, 6.0)
    queries = jnp.clip(queries, -6.0, 6.0)
    key_codes = jnp.clip(jax.random.normal(jax.random.fold_in(key, 102), (KEY_VALUE_HEADS, SEQUENCE_TOKENS, CHANNEL_DIM), jnp.float32), -6.0, 6.0)
    key_scale = jnp.exp(jax.random.uniform(jax.random.fold_in(key, 105), (KEY_VALUE_HEADS, SEQUENCE_TOKENS), jnp.float32, math.log(0.5), math.log(2.0)))
    value_scale = jnp.exp(jax.random.uniform(jax.random.fold_in(key, 106), (KEY_VALUE_HEADS, SEQUENCE_TOKENS), jnp.float32, math.log(0.5), math.log(2.0)))
    evict_flags = jax.random.randint(jax.random.fold_in(key, 107), (KEY_VALUE_HEADS, SEQUENCE_TOKENS), 0, 2, dtype=jnp.int32)
    return (queries.astype(jnp.bfloat16), key_codes.astype(jnp.bfloat16), key_scale, value_codes.astype(jnp.bfloat16), value_scale, evict_flags)


def forward_outputs(key):
    queries, key_codes, key_scale, value_codes, value_scale, evict_flags = base_inputs(key)
    group_width = ASKER_PROJ_NUM // KEY_VALUE_HEADS
    softmax_factor = CHANNEL_DIM ** (-0.5)
    ctx_count = SEQUENCE_TOKENS // TOK_DEV
    key_deq = (key_codes.astype(jnp.float32) * key_scale[:, :, None]).astype(jnp.bfloat16).astype(jnp.float32)
    value_deq = (value_codes.astype(jnp.float32) * value_scale[:, :, None]).astype(jnp.bfloat16).astype(jnp.float32)
    lookup_entry_list = jnp.repeat(key_deq, group_width, axis=0)
    payload_entry_list = jnp.repeat(value_deq, group_width, axis=0)
    evict_all = jnp.repeat(evict_flags, group_width, axis=0)
    key_pos = token_position_drawn(jnp.arange(SEQUENCE_TOKENS, dtype=jnp.int32), TOK_DEV, ctx_count)
    tile_span = math.gcd(SEQUENCE_TOKENS, 256)
    query_float = queries.astype(jnp.float32)

    def one_block(offset):
        query_block_rows = lax.dynamic_slice_in_dim(query_float, offset, tile_span, 0).reshape(tile_span, ASKER_PROJ_NUM, CHANNEL_DIM)
        query_pos = token_position_drawn(offset + jnp.arange(tile_span, dtype=jnp.int32), TOK_DEV, ctx_count)
        score_matrix = jnp.einsum('aps,prs->par', query_block_rows, lookup_entry_list) * softmax_factor
        distance = query_pos[:, None] - key_pos[None, :]
        visible = (distance[None] >= 0) & ((evict_all[:, None, :] == 0) | (distance[None] < DELAY))
        score_matrix = jnp.where(visible, score_matrix, -jnp.inf)
        highest = jnp.max(score_matrix, axis=2)
        natural_powers = jnp.exp(score_matrix - highest[:, :, None])
        cumulative_sums = jnp.sum(natural_powers, axis=2)
        norm_blk = highest + jnp.log(cumulative_sums)
        result_lines = jnp.einsum('djt,dti->jdi', natural_powers, payload_entry_list) / cumulative_sums.T[:, :, None]
        return (norm_blk, result_lines.reshape(tile_span, ASKER_PROJ_NUM * CHANNEL_DIM))
    block_starts = jnp.arange(0, SEQUENCE_TOKENS, tile_span, dtype=jnp.int32)
    norms, result_lines = lax.map(one_block, block_starts)
    log_norm = jnp.transpose(norms, (1, 0, 2)).reshape(ASKER_PROJ_NUM, SEQUENCE_TOKENS)
    return (log_norm, result_lines.reshape(SEQUENCE_TOKENS, ASKER_PROJ_NUM * CHANNEL_DIM).astype(jnp.bfloat16))


def draw_queries(key, part):
    return base_inputs(key)[0]


def draw_key_codes(key, part):
    return base_inputs(key)[1]


def draw_key_scale(key, part):
    return base_inputs(key)[2]


def draw_value_codes(key, part):
    return base_inputs(key)[3]


def draw_value_scale(key, part):
    return base_inputs(key)[4]


def draw_evict_flags(key, part):
    return base_inputs(key)[5]


def draw_log_norm(key, part):
    return forward_outputs(key)[0]


def draw_out_forward(key, part):
    return forward_outputs(key)[1]


def shard_levels(key, shape, shards, least, high):
    level, own = 1.0, jax.random.fold_in(key, 6)
    for dim, shards_of in shards:
        steps = jnp.exp(jax.random.uniform(jax.random.fold_in(own, dim), (shards_of,), jnp.float32, least / len(shards), high / len(shards)))
        level = level * jnp.repeat(steps, shape[dim] // shards_of).reshape([-1 if axis == dim else 1 for axis in range(len(shape))])
    return level


def centred(rng, extent, scale, limit, pieces=(), held_as=jnp.bfloat16):
    entries = jax.random.normal(rng, extent, jnp.float32) * scale
    if len(pieces) > 0:
        entries = shard_levels(rng, extent, pieces, -0.22, 0.18) * entries
    return jnp.clip(entries, min=-limit, max=limit).astype(held_as)


def setup_inputs(seed: int = 0) -> dict:
    arg_keys = jax.random.split(jax.random.key(seed), 10)
    return {
        "queries": draw_queries(jax.random.fold_in(arg_keys[9], 71), 0),
        "key_codes": draw_key_codes(jax.random.fold_in(arg_keys[9], 71), 0),
        "key_scale": draw_key_scale(jax.random.fold_in(arg_keys[9], 71), 0),
        "value_codes": draw_value_codes(jax.random.fold_in(arg_keys[9], 71), 0),
        "value_scale": draw_value_scale(jax.random.fold_in(arg_keys[9], 71), 0),
        "evict_flags": draw_evict_flags(jax.random.fold_in(arg_keys[9], 71), 0),
        "out_forward": draw_out_forward(jax.random.fold_in(arg_keys[9], 71), 0),
        "grad_output": centred(arg_keys[7], (SEQUENCE_TOKENS, ASKER_PROJ_NUM * CHANNEL_DIM), 1.0, 6.0, ((0, 64), (1, 8))),
        "log_norm": draw_log_norm(jax.random.fold_in(arg_keys[9], 71), 0),
    }


def rounded(values):
    return lax.optimization_barrier(values.astype(jnp.bfloat16)).astype(jnp.float32)


def token_position(rows, tok_dev, ctx_count):
    device_row = rows // tok_dev
    within = rows % tok_dev
    half = tok_dev // 2
    return jnp.where(within < half, device_row * half + within, (2 * ctx_count - 1 - device_row) * half + within - half).astype(jnp.int32)


def reference(queries, key_codes, key_scale, value_codes, value_scale, evict_flags, out_forward, grad_output, log_norm):
    group_width = ASKER_PROJ_NUM // KEY_VALUE_HEADS
    softmax_factor = CHANNEL_DIM ** -0.5
    ctx_count = SEQUENCE_TOKENS // TOK_DEV
    key_deq = rounded(key_codes.astype(jnp.float32) * key_scale[:, :, None])
    value_deq = rounded(value_codes.astype(jnp.float32) * value_scale[:, :, None])
    lookup_entry_list = jnp.repeat(key_deq, group_width, axis=0)
    payload_entry_list = jnp.repeat(value_deq, group_width, axis=0)
    evict_all = jnp.repeat(evict_flags, group_width, axis=0)
    products = grad_output.astype(jnp.float32) * out_forward.astype(jnp.float32)
    row_delta = jnp.sum(products.reshape(SEQUENCE_TOKENS, ASKER_PROJ_NUM, CHANNEL_DIM), axis=2).T
    key_pos = token_position(jnp.arange(SEQUENCE_TOKENS, dtype=jnp.int32), TOK_DEV, ctx_count)
    tile_span = math.gcd(SEQUENCE_TOKENS, 256)

    def one_block(running, offset):
        key_total, value_total = running
        query_block_rows = lax.dynamic_slice_in_dim(queries, offset, tile_span, 0).astype(jnp.float32).reshape(tile_span, ASKER_PROJ_NUM, CHANNEL_DIM)
        gradient_block = lax.dynamic_slice_in_dim(grad_output, offset, tile_span, 0).astype(jnp.float32).reshape(tile_span, ASKER_PROJ_NUM, CHANNEL_DIM)
        norm_blk = lax.dynamic_slice_in_dim(log_norm, offset, tile_span, 1)
        delta_blk = lax.dynamic_slice_in_dim(row_delta, offset, tile_span, 1)
        query_pos = token_position(offset + jnp.arange(tile_span, dtype=jnp.int32), TOK_DEV, ctx_count)
        score_matrix = jnp.einsum("aps,prs->par", query_block_rows, lookup_entry_list) * softmax_factor
        distance = query_pos[:, None] - key_pos[None, :]
        visible = (distance[None] >= 0) & ((evict_all[:, None, :] == 0) | (distance[None] < DELAY))
        attention_weights = jnp.where(visible, jnp.exp(score_matrix - norm_blk[:, :, None]), 0.0)
        weight_gradient = jnp.einsum("aps,prs->par", gradient_block, payload_entry_list)
        score_gradient = softmax_factor * attention_weights * (weight_gradient - delta_blk[:, :, None])
        weight_block = rounded(attention_weights)
        logit_derivative_tile = rounded(score_gradient)
        asker_derivative = jnp.einsum("djt,dti->jdi", logit_derivative_tile, lookup_entry_list).reshape(tile_span, ASKER_PROJ_NUM * CHANNEL_DIM).astype(jnp.bfloat16)
        key_portion = jnp.einsum("jqs,qjx->jsx", logit_derivative_tile, query_block_rows).reshape(KEY_VALUE_HEADS, group_width, SEQUENCE_TOKENS, CHANNEL_DIM).sum(axis=1)
        value_portion = jnp.einsum("jqs,qjx->jsx", weight_block, gradient_block).reshape(KEY_VALUE_HEADS, group_width, SEQUENCE_TOKENS, CHANNEL_DIM).sum(axis=1)
        return (key_total + key_portion, value_total + value_portion), asker_derivative

    block_starts = jnp.arange(0, SEQUENCE_TOKENS, tile_span, dtype=jnp.int32)
    empty = jnp.zeros((KEY_VALUE_HEADS, SEQUENCE_TOKENS, CHANNEL_DIM), jnp.float32)
    (key_total, value_total), query_grads = lax.scan(one_block, (empty, empty), block_starts)
    return (query_grads.reshape(SEQUENCE_TOKENS, ASKER_PROJ_NUM * CHANNEL_DIM), key_total.astype(jnp.bfloat16), value_total.astype(jnp.bfloat16))
```

```python
import functools
import math

import jax
import jax.numpy as jnp
from jax import lax
from jax.experimental import pallas as pl
from jax.experimental.pallas import tpu as pltpu
from jax.sharding import Mesh
from jax.sharding import PartitionSpec as P

DELAY = 256
HEAD = 128
TOK = 128
HALF = TOK // 2
YL, Z, CORE, YH, X = 2, 16, 2, 2, 4
CHIPS = YL * Z
SHARE = HALF // X
PEERS = CORE * X
BLOCKS = 2 * CHIPS * CORE
QROWS = 512
STAT = QROWS
QMSG = QROWS + 16
KROWS = 4 * SHARE
KMSG = KROWS + 8
TILE_SRC = CHIPS // 2
TILE = TILE_SRC * SHARE
QHALF = PEERS * TOK
SCALE = HEAD**-0.5
LOG2E = math.log2(math.e)
F32 = jnp.float32
BF16 = jnp.bfloat16
VMEM_SPEC = pl.BlockSpec(memory_space=pltpu.VMEM)


def split3(value):
    first = value.astype(BF16)
    rest = value - first.astype(F32)
    second = rest.astype(BF16)
    third = (rest - second.astype(F32)).astype(BF16)
    return [first, second, third]


def prep_kernel(q_ref, do_ref, out_ref, norm_ref, kc_ref, ks_ref, vc_ref, vs_ref, ev_ref, kmsg_ref, qmsg_ref):
    group = lax.axis_index("yh")
    part = lax.axis_index("x")

    def dequantized(code_ref, scale_ref, start):
        codes = code_ref[group, pl.ds(start, SHARE), :].astype(F32)
        scales = scale_ref[pl.ds(group, 1), :]
        lane = lax.broadcasted_iota(jnp.int32, (SHARE, TOK), 1)
        row = lax.broadcasted_iota(jnp.int32, (SHARE, TOK), 0) + start
        column = jnp.sum(jnp.where(lane == row, scales, 0.0), axis=1, keepdims=True)
        return (codes * column).astype(BF16)

    low = pl.multiple_of(part * SHARE, SHARE)
    high = pl.multiple_of(HALF + part * SHARE, SHARE)
    flags = jnp.broadcast_to(ev_ref[pl.ds(group, 1), :], (8, TOK)).astype(F32).astype(BF16)
    rows = jnp.concatenate(
        [
            dequantized(kc_ref, ks_ref, low),
            dequantized(kc_ref, ks_ref, high),
            dequantized(vc_ref, vs_ref, low),
            dequantized(vc_ref, vs_ref, high),
        ],
        axis=0,
    )
    for chip in range(CHIPS):
        kmsg_ref[chip, 0:KROWS, :] = rows
        kmsg_ref[chip, KROWS:KMSG, :] = flags

    q = q_ref[...]
    do = do_ref[...]
    product = do.astype(F32) * out_ref[...].astype(F32)
    norm = norm_ref[...] * LOG2E
    delta = jnp.concatenate(
        [jnp.sum(product[:, h * HEAD : (h + 1) * HEAD].T, axis=0, keepdims=True) for h in range(2)], axis=0
    )

    def halves(stat):
        return [
            jnp.concatenate([stat[0:1, b * HALF : (b + 1) * HALF], stat[1:2, b * HALF : (b + 1) * HALF]], axis=1)
            for b in range(2)
        ]

    norm_half, delta_half = halves(norm), halves(delta)
    stats = []
    for b in range(2):
        stats += split3(norm_half[b]) + split3(delta_half[b])
    stats = [s.astype(F32) for s in stats] + [jnp.zeros((4, TOK), F32)]
    stats = jnp.concatenate(stats, axis=0).astype(BF16)

    def reordered(value):
        return jnp.concatenate(
            [value[b * HALF : (b + 1) * HALF, h * HEAD : (h + 1) * HEAD] for b in range(2) for h in range(2)],
            axis=0,
        )

    qr = reordered(q)
    dr = reordered(do)
    for peer in range(PEERS):
        qmsg_ref[peer, 0:256, :] = qr
        qmsg_ref[peer, 256:512, :] = dr
        qmsg_ref[peer, QROWS:QMSG, :] = stats


def main_kernel(kmsg_ref, qmsg_ref, dkv_out, dq_out, dk_acc, dv_acc, dq_acc):
    chip = lax.axis_index("yl") * Z + lax.axis_index("z")
    core = lax.axis_index("core")
    part = lax.axis_index("x")
    dk_acc[...] = jnp.zeros_like(dk_acc)
    dv_acc[...] = jnp.zeros_like(dv_acc)
    dq_acc[...] = jnp.zeros_like(dq_acc)
    upper = (chip >= TILE_SRC).astype(jnp.int32)

    def key_info(tile):
        khalf = tile // 2
        src0 = TILE_SRC * jnp.where((tile == 1) | (tile == 2), 1, 0)
        index = lax.broadcasted_iota(jnp.int32, (TILE, 1), 0)
        src = src0 + index // SHARE
        block = jnp.where(khalf == 0, CORE * src + core, BLOCKS - 1 - CORE * src - core)
        offset = part * SHARE + index % SHARE
        pos = block * HALF + offset
        flags = kmsg_ref[pl.ds(src0, TILE_SRC), KROWS : KROWS + 8, :][:, 0, :].astype(F32)
        wide = jnp.broadcast_to(flags[:, None, :], (TILE_SRC, SHARE, TOK)).reshape(TILE, TOK)
        lane = lax.broadcasted_iota(jnp.int32, (TILE, TOK), 1)
        flag = jnp.sum(jnp.where(lane == khalf * HALF + offset, wide, 0.0), axis=1, keepdims=True)
        last = jnp.where(flag > 0.5, pos + DELAY - 1, BLOCKS * HALF)
        return khalf, src0, pos, last

    def stat_row(qhalf, which):
        rows = []
        base = STAT
        for peer in range(PEERS):
            both = qmsg_ref[peer, base : base + 16, :].astype(F32)
            def total(b):
                at = b * 6 + which * 3
                return both[at : at + 1] + both[at + 1 : at + 2] + both[at + 2 : at + 3]
            rows.append(jnp.where(qhalf == 0, total(0), total(1)))
        return jnp.concatenate(rows, axis=1)

    def pair(index, carry):
        is_low = (index == 4) | ((index == 3) & (upper == 1))
        qhalf = jnp.where(is_low, 0, 1)
        tile = jnp.where(index == 4, 0, jnp.where(is_low, 1, index))
        khalf, src0, kpos, klast = key_info(tile)
        krow = pl.multiple_of(khalf * SHARE, SHARE)
        vrow = pl.multiple_of(2 * SHARE + khalf * SHARE, SHARE)
        keys = kmsg_ref[pl.ds(src0, TILE_SRC), pl.ds(krow, SHARE), :].reshape(TILE, HEAD)
        values = kmsg_ref[pl.ds(src0, TILE_SRC), pl.ds(vrow, SHARE), :].reshape(TILE, HEAD)
        norm = stat_row(qhalf, 0)
        delta = stat_row(qhalf, 1)
        qi = lax.broadcasted_iota(jnp.int32, (1, QHALF), 1)
        qcore = qi // (X * TOK)
        qblock = jnp.where(is_low, CORE * chip + qcore, BLOCKS - 1 - CORE * chip - qcore)
        qpos = qblock * HALF + qi % HALF
        for sub in range(2):
            lo = sub * X
            q0 = pl.multiple_of(qhalf * TOK, TOK)
            d0 = pl.multiple_of(2 * TOK + qhalf * TOK, TOK)
            q = qmsg_ref[lo : lo + X, pl.ds(q0, TOK), :].reshape(X * TOK, HEAD)
            do = qmsg_ref[lo : lo + X, pl.ds(d0, TOK), :].reshape(X * TOK, HEAD)
            cut = slice(sub * X * TOK, (sub + 1) * X * TOK)
            s = lax.dot_general(keys, q, (((1,), (1,)), ((), ())), preferred_element_type=F32)
            dp = lax.dot_general(values, do, (((1,), (1,)), ((), ())), preferred_element_type=F32)
            seen = (kpos <= qpos[:, cut]) & (qpos[:, cut] <= klast)
            w = jnp.where(seen, jnp.exp2(s * (SCALE * LOG2E) - norm[:, cut]), 0.0)
            ds = ((w * SCALE) * (dp - delta[:, cut])).astype(BF16)
            wb = w.astype(BF16)
            dv_acc[tile] += jnp.dot(wb, do, preferred_element_type=F32)
            dk_acc[tile] += jnp.dot(ds, q, preferred_element_type=F32)
            dq_acc[qhalf, cut, :] += lax.dot_general(ds, keys, (((0,), (0,)), ((), ())), preferred_element_type=F32)
        return carry

    lax.fori_loop(0, 5, pair, 0)

    for tile in range(4):
        khalf = tile // 2
        s0 = TILE_SRC if tile in (1, 2) else 0
        dk = dk_acc[tile].astype(BF16).reshape(TILE_SRC, SHARE, HEAD)
        dv = dv_acc[tile].astype(BF16).reshape(TILE_SRC, SHARE, HEAD)
        dkv_out[s0 : s0 + TILE_SRC, khalf * SHARE : (khalf + 1) * SHARE, :] = dk
        dkv_out[s0 : s0 + TILE_SRC, (2 + khalf) * SHARE : (3 + khalf) * SHARE, :] = dv
    for peer in range(PEERS):
        for b in range(2):
            for h in range(2):
                r = peer * TOK + h * HALF
                dq_out[peer, b * HALF : (b + 1) * HALF, h * HEAD : (h + 1) * HEAD] = dq_acc[b, r : r + HALF, :].astype(BF16)


def dq_sum_kernel(in_ref, out_ref):
    total = in_ref[0].astype(F32)
    for peer in range(1, PEERS):
        total += in_ref[peer].astype(F32)
    out_ref[...] = total.astype(BF16)


def dkv_sum_kernel(in_ref, out_ref):
    total = in_ref[0].astype(F32)
    for chip in range(1, CHIPS):
        total += in_ref[chip].astype(F32)
    rows = total.astype(BF16)
    for peer in range(YH * X):
        out_ref[peer] = rows


def unpack_kernel(in_ref, dk_ref, dv_ref):
    for g in range(YH):
        for x in range(X):
            for b in range(2):
                at = b * HALF + x * SHARE
                dk_ref[g, at : at + SHARE, :] = in_ref[g * X + x, b * SHARE : (b + 1) * SHARE, :]
                dv_ref[g, at : at + SHARE, :] = in_ref[g * X + x, (2 + b) * SHARE : (3 + b) * SHARE, :]


def call(kernel, outs, n_in, name, scratch=(), flops=0, moved=1 << 20):
    shapes = tuple(jax.ShapeDtypeStruct(s, d) for s, d in outs)
    single = len(shapes) == 1
    return pl.pallas_call(
        kernel,
        out_shape=shapes[0] if single else shapes,
        in_specs=[VMEM_SPEC] * n_in,
        out_specs=VMEM_SPEC if single else (VMEM_SPEC,) * len(shapes),
        scratch_shapes=list(scratch),
        name=name,
        cost_estimate=pl.CostEstimate(flops=flops, bytes_accessed=moved, transcendentals=0),
    )


def exchange(value, axes):
    return lax.all_to_all(value, axes, 0, 0, tiled=True)


def local(queries, key_codes, key_scale, value_codes, value_scale, evict_flags, out_forward, grad_output, log_norm):
    kmsg, qmsg = call(prep_kernel, [((CHIPS, KMSG, HEAD), BF16), ((PEERS, QMSG, HEAD), BF16)], 9, "prep")(
        queries, grad_output, out_forward, log_norm, key_codes, key_scale, value_codes, value_scale, evict_flags
    )
    kall = exchange(kmsg, ("yl", "z"))
    qall = exchange(qmsg, ("core", "x"))
    dkv, dq = call(
        main_kernel,
        [((CHIPS, KROWS, HEAD), BF16), ((PEERS, TOK, 2 * HEAD), BF16)],
        2,
        "grads",
        scratch=[
            pltpu.VMEM((4, TILE, HEAD), F32),
            pltpu.VMEM((4, TILE, HEAD), F32),
            pltpu.VMEM((2, QHALF, HEAD), F32),
        ],
        flops=5 * 5 * 2 * TILE * QHALF * HEAD,
    )(kall, qall)
    dkv = exchange(dkv, ("yl", "z"))
    dq = exchange(dq, ("core", "x"))
    grad_queries = call(dq_sum_kernel, [((TOK, 2 * HEAD), BF16)], 1, "dq_sum")(dq)
    own = call(dkv_sum_kernel, [((YH * X, KROWS, HEAD), BF16)], 1, "dkv_sum")(dkv)
    every = exchange(own, ("yh", "x"))
    grad_keys, grad_values = call(unpack_kernel, [((2, TOK, HEAD), BF16)] * 2, 1, "unpack")(every)
    return grad_queries, grad_keys, grad_values


def solution(mesh):
    fine = Mesh(mesh.devices.reshape(YL, Z, CORE, YH, X), ("yl", "z", "core", "yh", "x"))
    ctx, head = ("yl", "z", "core"), ("yh", "x")
    in_specs = (
        P(ctx, head),
        P(None, ctx, None),
        P(None, ctx),
        P(None, ctx, None),
        P(None, ctx),
        P(None, ctx),
        P(ctx, head),
        P(ctx, head),
        P(head, ctx),
    )
    out_specs = (P(ctx, head), P(None, ctx, None), P(None, ctx, None))
    return jax.shard_map(local, mesh=fine, in_specs=in_specs, out_specs=out_specs, check_vma=False)
```

```python
import math

import jax
import jax.numpy as jnp
from jax import lax
from jax.experimental import pallas as pl
from jax.experimental.pallas import tpu as pltpu
from jax.sharding import Mesh
from jax.sharding import PartitionSpec as P


DELAY = 256
HEAD = 128
TOK = 128
HALF = TOK // 2
YL, Z, CORE, YH, X = 2, 16, 2, 2, 4
CHIPS = YL * Z
SHARE = HALF // X
PEERS = CORE * X
BLOCKS = 2 * CHIPS * CORE
QROWS = 512
STAT = QROWS
QMSG = QROWS + 16
KROWS = 4 * SHARE
KMSG = KROWS + 8
TILE_SRC = CHIPS // 2
TILE = TILE_SRC * SHARE
QHALF = PEERS * TOK
QSLOT = X * TOK
SCALE = HEAD**-0.5
LOG2E = math.log2(math.e)
F32 = jnp.float32
BF16 = jnp.bfloat16
VMEM_SPEC = pl.BlockSpec(memory_space=pltpu.VMEM)


def split3(value):
    first = value.astype(BF16)
    rest = value - first.astype(F32)
    second = rest.astype(BF16)
    third = (rest - second.astype(F32)).astype(BF16)
    return [first, second, third]


def prep_keys_kernel(kc_ref, ks_ref, vc_ref, vs_ref, ev_ref, kmsg_ref):
    group = lax.axis_index("yh")
    part = lax.axis_index("x")

    def dequantized(code_ref, scale_ref, start):
        codes = code_ref[group, pl.ds(start, SHARE), :].astype(F32)
        scales = scale_ref[pl.ds(group, 1), :]
        lane = lax.broadcasted_iota(jnp.int32, (SHARE, TOK), 1)
        row = lax.broadcasted_iota(jnp.int32, (SHARE, TOK), 0) + start
        column = jnp.sum(jnp.where(lane == row, scales, 0.0), axis=1, keepdims=True)
        return (codes * column).astype(BF16)

    low = pl.multiple_of(part * SHARE, SHARE)
    high = pl.multiple_of(HALF + part * SHARE, SHARE)
    flags = jnp.broadcast_to(ev_ref[pl.ds(group, 1), :], (8, TOK)).astype(F32).astype(BF16)
    rows = jnp.concatenate(
        [
            dequantized(kc_ref, ks_ref, low),
            dequantized(kc_ref, ks_ref, high),
            dequantized(vc_ref, vs_ref, low),
            dequantized(vc_ref, vs_ref, high),
        ],
        axis=0,
    )
    for peer in range(Z):
        kmsg_ref[peer, 0:KROWS, :] = rows
        kmsg_ref[peer, KROWS:KMSG, :] = flags


def prep_queries_kernel(q_ref, do_ref, out_ref, norm_ref, qmsg_ref):
    q = q_ref[...]
    do = do_ref[...]
    product = do.astype(F32) * out_ref[...].astype(F32)
    norm = norm_ref[...] * LOG2E
    delta = jnp.concatenate(
        [jnp.sum(product[:, h * HEAD : (h + 1) * HEAD].T, axis=0, keepdims=True) for h in range(2)], axis=0
    )

    def halves(stat):
        return [
            jnp.concatenate([stat[0:1, b * HALF : (b + 1) * HALF], stat[1:2, b * HALF : (b + 1) * HALF]], axis=1)
            for b in range(2)
        ]

    norm_half, delta_half = halves(norm), halves(delta)
    stats = []
    for b in range(2):
        stats += split3(norm_half[b]) + split3(delta_half[b])
    stats = [s.astype(F32) for s in stats] + [jnp.zeros((4, TOK), F32)]
    stats = jnp.concatenate(stats, axis=0).astype(BF16)

    def reordered(value):
        return jnp.concatenate(
            [value[b * HALF : (b + 1) * HALF, h * HEAD : (h + 1) * HEAD] for b in range(2) for h in range(2)],
            axis=0,
        )

    qmsg_ref[0:256, :] = reordered(q)
    qmsg_ref[256:512, :] = reordered(do)
    qmsg_ref[QROWS:QMSG, :] = stats


class Grads:
    def __init__(self, kmsg_ref, qmsg_refs, column, dk_acc, dv_acc):
        self.kmsg_ref, self.qmsg_refs, self.column = kmsg_ref, qmsg_refs, column
        self.dk_acc, self.dv_acc = dk_acc, dv_acc
        self.core = lax.axis_index("core")
        self.part = lax.axis_index("x")
        self.chip = lax.axis_index("yl") * Z + lax.axis_index("z")

    def keys(self, khalf):
        index = lax.broadcasted_iota(jnp.int32, (TILE, 1), 0)
        src = self.column * Z + index // SHARE
        block = jnp.where(khalf == 0, CORE * src + self.core, BLOCKS - 1 - CORE * src - self.core)
        offset = self.part * SHARE + index % SHARE
        pos = block * HALF + offset
        flags = self.kmsg_ref[:, KROWS : KROWS + 8, :][:, 0, :].astype(F32)
        wide = jnp.broadcast_to(flags[:, None, :], (Z, SHARE, TOK)).reshape(TILE, TOK)
        lane = lax.broadcasted_iota(jnp.int32, (TILE, TOK), 1)
        flag = jnp.sum(jnp.where(lane == khalf * HALF + offset, wide, 0.0), axis=1, keepdims=True)
        last = jnp.where(flag > 0.5, pos + DELAY - 1, BLOCKS * HALF)
        krow = pl.multiple_of(khalf * SHARE, SHARE)
        vrow = pl.multiple_of((2 + khalf) * SHARE, SHARE)
        k = self.kmsg_ref[:, pl.ds(krow, SHARE), :].reshape(TILE, HEAD)
        v = self.kmsg_ref[:, pl.ds(vrow, SHARE), :].reshape(TILE, HEAD)
        return k, v, pos, last

    def stat_row(self, qmsg_ref, qhalf, which):
        rows = []
        for peer in range(X):
            both = qmsg_ref[peer, STAT : STAT + 16, :].astype(F32)

            def total(b):
                at = b * 6 + which * 3
                return both[at : at + 1] + both[at + 1 : at + 2] + both[at + 2 : at + 3]

            rows.append(jnp.where(qhalf == 0, total(0), total(1)))
        return jnp.concatenate(rows, axis=1)

    def pair(self, qhalf, khalf, add_dq):
        k, v, kpos, klast = self.keys(khalf)
        q0 = pl.multiple_of(qhalf * TOK, TOK)
        d0 = pl.multiple_of((2 + qhalf) * TOK, TOK)
        for slot in range(CORE):
            qmsg_ref = self.qmsg_refs[slot]
            qcore = self.core if slot == 0 else 1 - self.core
            norm = self.stat_row(qmsg_ref, qhalf, 0)
            delta = self.stat_row(qmsg_ref, qhalf, 1)
            qblock = jnp.where(qhalf == 0, CORE * self.chip + qcore, BLOCKS - 1 - CORE * self.chip - qcore)
            qpos = qblock * HALF + lax.broadcasted_iota(jnp.int32, (1, QSLOT), 1) % HALF
            q = qmsg_ref[:, pl.ds(q0, TOK), :].reshape(QSLOT, HEAD)
            do = qmsg_ref[:, pl.ds(d0, TOK), :].reshape(QSLOT, HEAD)
            s = lax.dot_general(k, q, (((1,), (1,)), ((), ())), preferred_element_type=F32)
            dp = lax.dot_general(v, do, (((1,), (1,)), ((), ())), preferred_element_type=F32)
            seen = (kpos <= qpos) & (qpos <= klast)
            w = jnp.where(seen, jnp.exp2(s * (SCALE * LOG2E) - norm), 0.0)
            ds = ((w * SCALE) * (dp - delta)).astype(BF16)
            wb = w.astype(BF16)
            self.dv_acc[khalf] += jnp.dot(wb, do, preferred_element_type=F32)
            self.dk_acc[khalf] += jnp.dot(ds, q, preferred_element_type=F32)
            add_dq(slot, lax.dot_general(ds, k, (((0,), (0,)), ((), ())), preferred_element_type=F32))

    def write(self, out_ref, half):
        for khalf in range(2):
            dk = self.dk_acc[khalf].astype(BF16).reshape(Z, SHARE, HEAD)
            dv = self.dv_acc[khalf].astype(BF16).reshape(Z, SHARE, HEAD)
            out_ref[:, half, khalf * SHARE : (khalf + 1) * SHARE, :] = dk
            out_ref[:, half, (2 + khalf) * SHARE : (3 + khalf) * SHARE, :] = dv


def own_kernel(kmsg_ref, qmine_ref, qpeer_ref, dk_acc, dv_acc, dq_out):
    grads = Grads(kmsg_ref, (qmine_ref, qpeer_ref), lax.axis_index("yl"), dk_acc, dv_acc)
    dk_acc[...] = jnp.zeros_like(dk_acc)
    dv_acc[...] = jnp.zeros_like(dv_acc)
    dq_out[...] = jnp.zeros_like(dq_out)
    for qhalf, khalf in ((0, 0), (1, 0), (1, 1)):

        def add(slot, value, qhalf=qhalf):
            dq_out[qhalf, slot] += value

        grads.pair(qhalf, khalf, add)


def other_kernel(
    kmsg_ref, qmine_ref, qpeer_ref, dk_ref, dv_ref, dq_ref, dkv_out, keep_out, send_out, dk_acc, dv_acc, dq_acc
):
    column = lax.axis_index("yl")
    queries = (qmine_ref, qpeer_ref)
    grads = Grads(kmsg_ref, queries, 1 - column, dk_acc, dv_acc)
    dk_acc[...] = jnp.zeros_like(dk_acc)
    dv_acc[...] = jnp.zeros_like(dv_acc)
    dq_acc[...] = dq_ref[...]

    def add_high(slot, value):
        dq_acc[1, slot] += value

    grads.pair(1, 0, add_high)
    half = 1 - column

    def add_half(slot, value):
        dq_acc[half, slot] += value

    grads.pair(half, half, add_half)
    grads.write(dkv_out, 1)
    Grads(kmsg_ref, queries, column, dk_ref, dv_ref).write(dkv_out, 0)
    for slot, out in ((0, keep_out), (1, send_out)):
        for peer in range(X):
            for b in range(2):
                for h in range(2):
                    r = peer * TOK + h * HALF
                    out[peer, b * HALF : (b + 1) * HALF, h * HEAD : (h + 1) * HEAD] = dq_acc[b, slot, r : r + HALF, :]


def dq_add_kernel(keep_ref, got_ref, *out_refs):
    part = lax.axis_index("x")
    for shift in range(X):
        to = (part + shift) % X
        out_refs[shift][...] = keep_ref[to] + got_ref[to]


def dq_sum_kernel(*refs):
    *in_refs, out_ref = refs
    total = in_refs[0][...]
    for ref in in_refs[1:]:
        total += ref[...]
    out_ref[...] = total.astype(BF16)


def dkv_sum_kernel(in_ref, out_ref):
    column = lax.axis_index("yl")
    for half in range(YL):
        total = in_ref[0, half].astype(F32)
        for peer in range(1, Z):
            total += in_ref[peer, half].astype(F32)
        to = column if half == 0 else 1 - column
        for peer in range(YH * X):
            out_ref[to * YH * X + peer] = total


def unpack_kernel(in_ref, dk_ref, dv_ref):
    for g in range(YH):
        for x in range(X):
            rows = (in_ref[g * X + x] + in_ref[YH * X + g * X + x]).astype(BF16)
            for b in range(2):
                at = b * HALF + x * SHARE
                dk_ref[g, at : at + SHARE, :] = rows[b * SHARE : (b + 1) * SHARE, :]
                dv_ref[g, at : at + SHARE, :] = rows[(2 + b) * SHARE : (3 + b) * SHARE, :]


def call(kernel, outs, n_in, scratch=(), flops=0, moved=1 << 20, vmem=8):
    shapes = tuple(jax.ShapeDtypeStruct(s, d) for s, d in outs)
    single = len(shapes) == 1
    return pl.pallas_call(
        kernel,
        out_shape=shapes[0] if single else shapes,
        in_specs=[VMEM_SPEC] * n_in,
        out_specs=VMEM_SPEC if single else (VMEM_SPEC,) * len(shapes),
        scratch_shapes=list(scratch),
        compiler_params=pltpu.CompilerParams(vmem_limit_bytes=vmem << 20),
        cost_estimate=pl.CostEstimate(flops=flops, bytes_accessed=moved, transcendentals=0),
    )


def exchange(value, axes):
    return lax.all_to_all(value, axes, 0, 0, tiled=True)


def shifted(value, axis, size, shift):
    return lax.ppermute(value, axis, [(i, (i + shift) % size) for i in range(size)])


def local(queries, key_codes, key_scale, value_codes, value_scale, evict_flags, out_forward, grad_output, log_norm):
    kmsg = call(prep_keys_kernel, [((Z, KMSG, HEAD), BF16)], 5, vmem=56)(
        key_codes, key_scale, value_codes, value_scale, evict_flags
    )
    kown = exchange(kmsg, "z")
    qmsg = call(prep_queries_kernel, [((QMSG, HEAD), BF16)], 4, vmem=56)(queries, grad_output, out_forward, log_norm)
    qmine = lax.all_gather(qmsg, "x", axis=0)
    qpeer = shifted(qmine, "core", CORE, 1)
    kother = shifted(kown, "yl", YL, 1)
    work = 5 * 2 * TILE * QHALF * HEAD
    acc = ((2, TILE, HEAD), F32)
    dq_acc = ((2, CORE, QSLOT, HEAD), F32)
    piece = ((X, TOK, 2 * HEAD), F32)
    dk_own, dv_own, dq_own = call(own_kernel, [acc, acc, dq_acc], 3, flops=3 * work, vmem=24)(kown, qmine, qpeer)
    dkv, keep, send = call(
        other_kernel,
        [((Z, YL, KROWS, HEAD), BF16), piece, piece],
        6,
        scratch=[pltpu.VMEM(*acc), pltpu.VMEM(*acc), pltpu.VMEM(*dq_acc)],
        flops=2 * work,
        vmem=24,
    )(kother, qmine, qpeer, dk_own, dv_own, dq_own)
    dkv = exchange(dkv, "z")
    got = shifted(send, "core", CORE, 1)
    parts = call(dq_add_kernel, [((TOK, 2 * HEAD), F32)] * X, 2)(keep, got)
    parts = [parts[0]] + [shifted(parts[k], "x", X, k) for k in range(1, X)]
    grad_queries = call(dq_sum_kernel, [((TOK, 2 * HEAD), BF16)], X)(*parts)
    both = call(dkv_sum_kernel, [((YL * YH * X, KROWS, HEAD), F32)], 1)(dkv)
    every = exchange(both, ("yl", "yh", "x"))
    grad_keys, grad_values = call(unpack_kernel, [((2, TOK, HEAD), BF16)] * 2, 1)(every)
    return grad_queries, grad_keys, grad_values


def solution(mesh):
    fine = Mesh(mesh.devices.reshape(YL, Z, CORE, YH, X), ("yl", "z", "core", "yh", "x"))
    ctx, head = ("yl", "z", "core"), ("yh", "x")
    in_specs = (
        P(ctx, head),
        P(None, ctx, None),
        P(None, ctx),
        P(None, ctx, None),
        P(None, ctx),
        P(None, ctx),
        P(ctx, head),
        P(ctx, head),
        P(head, ctx),
    )
    out_specs = (P(ctx, head), P(None, ctx, None), P(None, ctx, None))
    return jax.shard_map(local, mesh=fine, in_specs=in_specs, out_specs=out_specs, check_vma=False)
```

```python
import math

import jax
import jax.numpy as jnp
from jax import lax
from jax.experimental import pallas as pl
from jax.experimental.pallas import tpu as pltpu
from jax.sharding import Mesh
from jax.sharding import PartitionSpec as P


DELAY = 256
HEAD = 128
TOK = 128
HALF = TOK // 2
YL, Z, CORE, YH, X = 2, 16, 2, 2, 4
CHIPS = YL * Z
SHARE = HALF // X
PEERS = CORE * X
BLOCKS = 2 * CHIPS * CORE
QROWS = 512
STAT = QROWS
QMSG = QROWS + 16
KROWS = 4 * SHARE
KMSG = KROWS + 8
TILE_SRC = CHIPS // 2
TILE = TILE_SRC * SHARE
QHALF = PEERS * TOK
QSLOT = X * TOK
SCALE = HEAD**-0.5
LOG2E = math.log2(math.e)
F32 = jnp.float32
BF16 = jnp.bfloat16
VMEM_SPEC = pl.BlockSpec(memory_space=pltpu.VMEM)


def split3(value):
    first = value.astype(BF16)
    rest = value - first.astype(F32)
    second = rest.astype(BF16)
    third = (rest - second.astype(F32)).astype(BF16)
    return [first, second, third]


def prep_keys_kernel(kc_ref, ks_ref, vc_ref, vs_ref, ev_ref, kmsg_ref):
    group = lax.axis_index("yh")
    part = lax.axis_index("x")

    def dequantized(code_ref, scale_ref, start):
        codes = code_ref[group, pl.ds(start, SHARE), :].astype(F32)
        scales = scale_ref[pl.ds(group, 1), :]
        lane = lax.broadcasted_iota(jnp.int32, (SHARE, TOK), 1)
        row = lax.broadcasted_iota(jnp.int32, (SHARE, TOK), 0) + start
        column = jnp.sum(jnp.where(lane == row, scales, 0.0), axis=1, keepdims=True)
        return (codes * column).astype(BF16)

    low = pl.multiple_of(part * SHARE, SHARE)
    high = pl.multiple_of(HALF + part * SHARE, SHARE)
    flags = jnp.broadcast_to(ev_ref[pl.ds(group, 1), :], (8, TOK)).astype(F32).astype(BF16)
    rows = jnp.concatenate(
        [
            dequantized(kc_ref, ks_ref, low),
            dequantized(kc_ref, ks_ref, high),
            dequantized(vc_ref, vs_ref, low),
            dequantized(vc_ref, vs_ref, high),
        ],
        axis=0,
    )
    kmsg_ref[0:KROWS, :] = rows
    kmsg_ref[KROWS:KMSG, :] = flags


def spread_kernel(own_ref, other_ref, out_ref):
    own, other = own_ref[...], other_ref[...]
    for peer in range(Z):
        out_ref[peer, 0:KMSG, :] = own
        out_ref[peer, KMSG : 2 * KMSG, :] = other


def stack_kernel(*refs):
    *in_refs, out_ref = refs
    for slot, ref in enumerate(in_refs):
        out_ref[slot] = ref[...]


def prep_queries_kernel(q_ref, do_ref, out_ref, norm_ref, qmsg_ref):
    q = q_ref[...]
    do = do_ref[...]
    product = do.astype(F32) * out_ref[...].astype(F32)
    norm = norm_ref[...] * LOG2E
    delta = jnp.concatenate(
        [jnp.sum(product[:, h * HEAD : (h + 1) * HEAD].T, axis=0, keepdims=True) for h in range(2)], axis=0
    )

    def halves(stat):
        return [
            jnp.concatenate([stat[0:1, b * HALF : (b + 1) * HALF], stat[1:2, b * HALF : (b + 1) * HALF]], axis=1)
            for b in range(2)
        ]

    norm_half, delta_half = halves(norm), halves(delta)
    stats = []
    for b in range(2):
        stats += split3(norm_half[b]) + split3(delta_half[b])
    stats = [s.astype(F32) for s in stats] + [jnp.zeros((4, TOK), F32)]
    stats = jnp.concatenate(stats, axis=0).astype(BF16)

    def reordered(value):
        return jnp.concatenate(
            [value[b * HALF : (b + 1) * HALF, h * HEAD : (h + 1) * HEAD] for b in range(2) for h in range(2)],
            axis=0,
        )

    qmsg_ref[0:256, :] = reordered(q)
    qmsg_ref[256:512, :] = reordered(do)
    qmsg_ref[QROWS:QMSG, :] = stats


class Grads:
    def __init__(self, kmsg_ref, qmsg_refs, half, dk_acc, dv_acc):
        self.kmsg_ref, self.qmsg_refs, self.base = kmsg_ref, qmsg_refs, half * KMSG
        self.dk_acc, self.dv_acc = dk_acc, dv_acc
        self.core = lax.axis_index("core")
        self.part = lax.axis_index("x")
        own = lax.axis_index("yl")
        self.chip = own * Z + lax.axis_index("z")
        self.column = own if half == 0 else 1 - own

    def keys(self, khalf):
        index = lax.broadcasted_iota(jnp.int32, (TILE, 1), 0)
        src = self.column * Z + index // SHARE
        block = jnp.where(khalf == 0, CORE * src + self.core, BLOCKS - 1 - CORE * src - self.core)
        offset = self.part * SHARE + index % SHARE
        pos = block * HALF + offset
        at = self.base + KROWS
        flags = self.kmsg_ref[:, at : at + 8, :][:, 0, :].astype(F32)
        wide = jnp.broadcast_to(flags[:, None, :], (Z, SHARE, TOK)).reshape(TILE, TOK)
        lane = lax.broadcasted_iota(jnp.int32, (TILE, TOK), 1)
        flag = jnp.sum(jnp.where(lane == khalf * HALF + offset, wide, 0.0), axis=1, keepdims=True)
        last = jnp.where(flag > 0.5, pos + DELAY - 1, BLOCKS * HALF)
        krow = pl.multiple_of(self.base + khalf * SHARE, 8)
        vrow = pl.multiple_of(self.base + (2 + khalf) * SHARE, 8)
        k = self.kmsg_ref[:, pl.ds(krow, SHARE), :].reshape(TILE, HEAD)
        v = self.kmsg_ref[:, pl.ds(vrow, SHARE), :].reshape(TILE, HEAD)
        return k, v, pos, last

    def stat_row(self, qmsg_ref, qhalf, which):
        rows = []
        for peer in range(X):
            both = qmsg_ref[peer, STAT : STAT + 16, :].astype(F32)

            def total(b):
                at = b * 6 + which * 3
                return both[at : at + 1] + both[at + 1 : at + 2] + both[at + 2 : at + 3]

            rows.append(jnp.where(qhalf == 0, total(0), total(1)))
        return jnp.concatenate(rows, axis=1)

    def pair(self, qhalf, khalf, add_dq):
        k, v, kpos, klast = self.keys(khalf)
        q0 = pl.multiple_of(qhalf * TOK, TOK)
        d0 = pl.multiple_of((2 + qhalf) * TOK, TOK)
        for slot in range(CORE):
            qmsg_ref = self.qmsg_refs[slot]
            qcore = self.core if slot == 0 else 1 - self.core
            norm = self.stat_row(qmsg_ref, qhalf, 0)
            delta = self.stat_row(qmsg_ref, qhalf, 1)
            qblock = jnp.where(qhalf == 0, CORE * self.chip + qcore, BLOCKS - 1 - CORE * self.chip - qcore)
            qpos = qblock * HALF + lax.broadcasted_iota(jnp.int32, (1, QSLOT), 1) % HALF
            q = qmsg_ref[:, pl.ds(q0, TOK), :].reshape(QSLOT, HEAD)
            do = qmsg_ref[:, pl.ds(d0, TOK), :].reshape(QSLOT, HEAD)
            s = lax.dot_general(k, q, (((1,), (1,)), ((), ())), preferred_element_type=F32)
            dp = lax.dot_general(v, do, (((1,), (1,)), ((), ())), preferred_element_type=F32)
            seen = (kpos <= qpos) & (qpos <= klast)
            w = jnp.where(seen, jnp.exp2(s * (SCALE * LOG2E) - norm), 0.0)
            ds = ((w * SCALE) * (dp - delta)).astype(BF16)
            wb = w.astype(BF16)
            self.dv_acc[khalf] += jnp.dot(wb, do, preferred_element_type=F32)
            self.dk_acc[khalf] += jnp.dot(ds, q, preferred_element_type=F32)
            add_dq(slot, lax.dot_general(ds, k, (((0,), (0,)), ((), ())), preferred_element_type=F32))

    def write(self, out_ref, half):
        for khalf in range(2):
            dk = self.dk_acc[khalf].astype(BF16).reshape(Z, SHARE, HEAD)
            dv = self.dv_acc[khalf].astype(BF16).reshape(Z, SHARE, HEAD)
            out_ref[:, half, khalf * SHARE : (khalf + 1) * SHARE, :] = dk
            out_ref[:, half, (2 + khalf) * SHARE : (3 + khalf) * SHARE, :] = dv


def grads_kernel(kmsg_ref, qmine_ref, qpeer_ref, dkv_out, keep_out, send_out, dk_acc, dv_acc, dq_acc):
    queries = (qmine_ref, qpeer_ref)
    dk_acc[...] = jnp.zeros_like(dk_acc)
    dv_acc[...] = jnp.zeros_like(dv_acc)
    dq_acc[...] = jnp.zeros_like(dq_acc)
    rest = 1 - lax.axis_index("yl")
    for half, pairs in ((0, ((0, 0), (1, 0), (1, 1))), (1, ((1, 0), (rest, rest)))):
        grads = Grads(kmsg_ref, queries, half, dk_acc.at[half], dv_acc.at[half])
        for qhalf, khalf in pairs:

            def add(slot, value, qhalf=qhalf):
                dq_acc[qhalf, slot] += value

            grads.pair(qhalf, khalf, add)
        grads.write(dkv_out, half)
    for slot, out in ((0, keep_out), (1, send_out)):
        for peer in range(X):
            for b in range(2):
                for h in range(2):
                    r = peer * TOK + h * HALF
                    out[peer, b * HALF : (b + 1) * HALF, h * HEAD : (h + 1) * HEAD] = dq_acc[b, slot, r : r + HALF, :]


def dq_add_kernel(keep_ref, got_ref, *out_refs):
    for slot in range(X):
        out_refs[slot][...] = keep_ref[slot] + got_ref[slot]


def dq_sum_kernel(*refs):
    *in_refs, out_ref = refs
    total = in_refs[0][...]
    for ref in in_refs[1:]:
        total += ref[...]
    out_ref[...] = total.astype(BF16)


def dkv_sum_kernel(in_ref, out_ref):
    column = lax.axis_index("yl")
    for half in range(YL):
        total = in_ref[0, half].astype(F32)
        for peer in range(1, Z):
            total += in_ref[peer, half].astype(F32)
        to = column if half == 0 else 1 - column
        for peer in range(YH * X):
            out_ref[to * YH * X + peer] = total


def unpack_kernel(in_ref, dk_ref, dv_ref):
    for g in range(YH):
        for x in range(X):
            rows = (in_ref[g * X + x] + in_ref[YH * X + g * X + x]).astype(BF16)
            for b in range(2):
                at = b * HALF + x * SHARE
                dk_ref[g, at : at + SHARE, :] = rows[b * SHARE : (b + 1) * SHARE, :]
                dv_ref[g, at : at + SHARE, :] = rows[(2 + b) * SHARE : (3 + b) * SHARE, :]


def call(kernel, outs, n_in, scratch=(), flops=0, moved=1 << 20, vmem=8):
    shapes = tuple(jax.ShapeDtypeStruct(s, d) for s, d in outs)
    single = len(shapes) == 1
    return pl.pallas_call(
        kernel,
        out_shape=shapes[0] if single else shapes,
        in_specs=[VMEM_SPEC] * n_in,
        out_specs=VMEM_SPEC if single else (VMEM_SPEC,) * len(shapes),
        scratch_shapes=list(scratch),
        compiler_params=pltpu.CompilerParams(vmem_limit_bytes=vmem << 20),
        cost_estimate=pl.CostEstimate(flops=flops, bytes_accessed=moved, transcendentals=0),
    )


def exchange(value, axes):
    return lax.all_to_all(value, axes, 0, 0, tiled=True)


def shifted(value, axis, size, shift):
    return lax.ppermute(value, axis, [(i, (i + shift) % size) for i in range(size)])


def local(queries, key_codes, key_scale, value_codes, value_scale, evict_flags, out_forward, grad_output, log_norm):
    kmsg = call(prep_keys_kernel, [((KMSG, HEAD), BF16)], 5, vmem=56)(
        key_codes, key_scale, value_codes, value_scale, evict_flags
    )
    kother = shifted(kmsg, "yl", YL, 1)
    qmsg = call(prep_queries_kernel, [((QMSG, HEAD), BF16)], 4, vmem=56)(queries, grad_output, out_forward, log_norm)
    kmsg = call(spread_kernel, [((Z, YL * KMSG, HEAD), BF16)], 2)(kmsg, kother)
    kall = exchange(kmsg, "z")
    slots = [qmsg]
    for k in range(1, X):
        slots.append(shifted(qmsg, "x", X, k))
    qmine = call(stack_kernel, [((X, QMSG, HEAD), BF16)], X)(*slots)
    qpeer = shifted(qmine, "core", CORE, 1)
    acc = pltpu.VMEM((YL, 2, TILE, HEAD), F32)
    piece = ((X, TOK, 2 * HEAD), F32)
    dkv, keep, send = call(
        grads_kernel,
        [((Z, YL, KROWS, HEAD), BF16), piece, piece],
        3,
        scratch=[acc, acc, pltpu.VMEM((2, CORE, QSLOT, HEAD), F32)],
        flops=25 * 2 * TILE * QHALF * HEAD,
        vmem=24,
    )(kall, qmine, qpeer)
    dkv = exchange(dkv, "z")
    got = shifted(send, "core", CORE, 1)
    parts = call(dq_add_kernel, [((TOK, 2 * HEAD), F32)] * X, 2)(keep, got)
    home = [parts[0]]
    for k in range(1, X):
        home.append(shifted(parts[k], "x", X, X - k))
    grad_queries = call(dq_sum_kernel, [((TOK, 2 * HEAD), BF16)], X)(*home)
    both = call(dkv_sum_kernel, [((YL * YH * X, KROWS, HEAD), F32)], 1)(dkv)
    every = exchange(both, ("yl", "yh", "x"))
    grad_keys, grad_values = call(unpack_kernel, [((2, TOK, HEAD), BF16)] * 2, 1)(every)
    return grad_queries, grad_keys, grad_values


def solution(mesh):
    fine = Mesh(mesh.devices.reshape(YL, Z, CORE, YH, X), ("yl", "z", "core", "yh", "x"))
    ctx, head = ("yl", "z", "core"), ("yh", "x")
    in_specs = (
        P(ctx, head),
        P(None, ctx, None),
        P(None, ctx),
        P(None, ctx, None),
        P(None, ctx),
        P(None, ctx),
        P(ctx, head),
        P(ctx, head),
        P(head, ctx),
    )
    out_specs = (P(ctx, head), P(None, ctx, None), P(None, ctx, None))
    return jax.shard_map(local, mesh=fine, in_specs=in_specs, out_specs=out_specs, check_vma=False)
```

```python
import math

import jax
import jax.numpy as jnp
from jax import lax
from jax.experimental import pallas as pl
from jax.experimental.pallas import tpu as pltpu
from jax.sharding import Mesh
from jax.sharding import PartitionSpec as P


DELAY = 256
HEAD = 128
TOK = 128
HALF = TOK // 2
YL, Z, CORE, YH, X = 2, 16, 2, 2, 4
CHIPS = YL * Z
SHARE = HALF // X
PEERS = CORE * X
BLOCKS = 2 * CHIPS * CORE
QROWS = 512
STAT = QROWS
QMSG = QROWS + 16
KROWS = 4 * SHARE
KMSG = KROWS + 8
TILE_SRC = CHIPS // 2
TILE = TILE_SRC * SHARE
QHALF = PEERS * TOK
QSLOT = X * TOK
SCALE = HEAD**-0.5
LOG2E = math.log2(math.e)
F32 = jnp.float32
BF16 = jnp.bfloat16
VMEM_SPEC = pl.BlockSpec(memory_space=pltpu.VMEM)


def split3(value):
    first = value.astype(BF16)
    rest = value - first.astype(F32)
    second = rest.astype(BF16)
    third = (rest - second.astype(F32)).astype(BF16)
    return [first, second, third]


def prep_keys_kernel(kc_ref, ks_ref, vc_ref, vs_ref, ev_ref, kmsg_ref):
    group = lax.axis_index("yh")
    part = lax.axis_index("x")

    def dequantized(code_ref, scale_ref, start):
        codes = code_ref[group, pl.ds(start, SHARE), :].astype(F32)
        scales = scale_ref[pl.ds(group, 1), :]
        lane = lax.broadcasted_iota(jnp.int32, (SHARE, TOK), 1)
        row = lax.broadcasted_iota(jnp.int32, (SHARE, TOK), 0) + start
        column = jnp.sum(jnp.where(lane == row, scales, 0.0), axis=1, keepdims=True)
        return (codes * column).astype(BF16)

    low = pl.multiple_of(part * SHARE, SHARE)
    high = pl.multiple_of(HALF + part * SHARE, SHARE)
    flags = jnp.broadcast_to(ev_ref[pl.ds(group, 1), :], (8, TOK)).astype(F32).astype(BF16)
    rows = jnp.concatenate(
        [
            dequantized(kc_ref, ks_ref, low),
            dequantized(kc_ref, ks_ref, high),
            dequantized(vc_ref, vs_ref, low),
            dequantized(vc_ref, vs_ref, high),
        ],
        axis=0,
    )
    for peer in range(Z):
        kmsg_ref[peer, 0:KROWS, :] = rows
        kmsg_ref[peer, KROWS:KMSG, :] = flags


def prep_queries_kernel(q_ref, do_ref, out_ref, norm_ref, qmsg_ref):
    q = q_ref[...]
    do = do_ref[...]
    product = do.astype(F32) * out_ref[...].astype(F32)
    norm = norm_ref[...] * LOG2E
    delta = jnp.concatenate(
        [jnp.sum(product[:, h * HEAD : (h + 1) * HEAD].T, axis=0, keepdims=True) for h in range(2)], axis=0
    )

    def halves(stat):
        return [
            jnp.concatenate([stat[0:1, b * HALF : (b + 1) * HALF], stat[1:2, b * HALF : (b + 1) * HALF]], axis=1)
            for b in range(2)
        ]

    norm_half, delta_half = halves(norm), halves(delta)
    stats = []
    for b in range(2):
        stats += split3(norm_half[b]) + split3(delta_half[b])
    stats = [s.astype(F32) for s in stats] + [jnp.zeros((4, TOK), F32)]
    stats = jnp.concatenate(stats, axis=0).astype(BF16)

    def reordered(value):
        return jnp.concatenate(
            [value[b * HALF : (b + 1) * HALF, h * HEAD : (h + 1) * HEAD] for b in range(2) for h in range(2)],
            axis=0,
        )

    qmsg_ref[0:256, :] = reordered(q)
    qmsg_ref[256:512, :] = reordered(do)
    qmsg_ref[QROWS:QMSG, :] = stats


class Grads:
    def __init__(self, kmsg_ref, qmsg_refs, other, dk_acc, dv_acc):
        self.kmsg_ref, self.qmsg_refs = kmsg_ref, qmsg_refs
        self.dk_acc, self.dv_acc = dk_acc, dv_acc
        self.core = lax.axis_index("core")
        self.part = lax.axis_index("x")
        own = lax.axis_index("yl")
        self.chip = own * Z + lax.axis_index("z")
        self.column = 1 - own if other else own
        dk_acc[...] = jnp.zeros_like(dk_acc)
        dv_acc[...] = jnp.zeros_like(dv_acc)

    def keys(self, khalf):
        index = lax.broadcasted_iota(jnp.int32, (TILE, 1), 0)
        src = self.column * Z + index // SHARE
        block = jnp.where(khalf == 0, CORE * src + self.core, BLOCKS - 1 - CORE * src - self.core)
        offset = self.part * SHARE + index % SHARE
        pos = block * HALF + offset
        flags = self.kmsg_ref[:, KROWS : KROWS + 8, :][:, 0, :].astype(F32)
        wide = jnp.broadcast_to(flags[:, None, :], (Z, SHARE, TOK)).reshape(TILE, TOK)
        lane = lax.broadcasted_iota(jnp.int32, (TILE, TOK), 1)
        flag = jnp.sum(jnp.where(lane == khalf * HALF + offset, wide, 0.0), axis=1, keepdims=True)
        last = jnp.where(flag > 0.5, pos + DELAY - 1, BLOCKS * HALF)
        krow = pl.multiple_of(khalf * SHARE, SHARE)
        vrow = pl.multiple_of((2 + khalf) * SHARE, SHARE)
        k = self.kmsg_ref[:, pl.ds(krow, SHARE), :].reshape(TILE, HEAD)
        v = self.kmsg_ref[:, pl.ds(vrow, SHARE), :].reshape(TILE, HEAD)
        return k, v, pos, last

    def stat_row(self, qmsg_ref, qhalf, which):
        rows = []
        for peer in range(X):
            both = qmsg_ref[peer, STAT : STAT + 16, :].astype(F32)

            def total(b):
                at = b * 6 + which * 3
                return both[at : at + 1] + both[at + 1 : at + 2] + both[at + 2 : at + 3]

            rows.append(jnp.where(qhalf == 0, total(0), total(1)))
        return jnp.concatenate(rows, axis=1)

    def pair(self, qhalf, khalf, add_dq):
        k, v, kpos, klast = self.keys(khalf)
        q0 = pl.multiple_of(qhalf * TOK, TOK)
        d0 = pl.multiple_of((2 + qhalf) * TOK, TOK)
        for slot in range(CORE):
            qmsg_ref = self.qmsg_refs[slot]
            qcore = self.core if slot == 0 else 1 - self.core
            norm = self.stat_row(qmsg_ref, qhalf, 0)
            delta = self.stat_row(qmsg_ref, qhalf, 1)
            qblock = jnp.where(qhalf == 0, CORE * self.chip + qcore, BLOCKS - 1 - CORE * self.chip - qcore)
            qpos = qblock * HALF + lax.broadcasted_iota(jnp.int32, (1, QSLOT), 1) % HALF
            q = qmsg_ref[:, pl.ds(q0, TOK), :].reshape(QSLOT, HEAD)
            do = qmsg_ref[:, pl.ds(d0, TOK), :].reshape(QSLOT, HEAD)
            s = lax.dot_general(k, q, (((1,), (1,)), ((), ())), preferred_element_type=F32)
            dp = lax.dot_general(v, do, (((1,), (1,)), ((), ())), preferred_element_type=F32)
            seen = (kpos <= qpos) & (qpos <= klast)
            w = jnp.where(seen, jnp.exp2(s * (SCALE * LOG2E) - norm), 0.0)
            ds = ((w * SCALE) * (dp - delta)).astype(BF16)
            wb = w.astype(BF16)
            self.dv_acc[khalf] += jnp.dot(wb, do, preferred_element_type=F32)
            self.dk_acc[khalf] += jnp.dot(ds, q, preferred_element_type=F32)
            add_dq(slot, lax.dot_general(ds, k, (((0,), (0,)), ((), ())), preferred_element_type=F32))

    def write(self, out_ref):
        for khalf in range(2):
            dk = self.dk_acc[khalf].reshape(Z, SHARE, HEAD)
            dv = self.dv_acc[khalf].reshape(Z, SHARE, HEAD)
            out_ref[:, khalf * SHARE : (khalf + 1) * SHARE, :] = dk
            out_ref[:, (2 + khalf) * SHARE : (3 + khalf) * SHARE, :] = dv


def other_kernel(kmsg_ref, qmine_ref, qpeer_ref, dkv_out, dq_out, dk_acc, dv_acc):
    grads = Grads(kmsg_ref, (qmine_ref, qpeer_ref), True, dk_acc, dv_acc)
    dq_out[...] = jnp.zeros_like(dq_out)
    rest = 1 - lax.axis_index("yl")
    for qhalf, khalf in ((1, 0), (rest, rest)):

        def add(slot, value, qhalf=qhalf):
            dq_out[qhalf, slot] += value

        grads.pair(qhalf, khalf, add)
    grads.write(dkv_out)


def own_kernel(kmsg_ref, qmine_ref, qpeer_ref, dq_ref, dkv_out, keep_out, send_out, dk_acc, dv_acc, dq_acc):
    grads = Grads(kmsg_ref, (qmine_ref, qpeer_ref), False, dk_acc, dv_acc)
    dq_acc[...] = dq_ref[...]
    for qhalf, khalf in ((0, 0), (1, 0), (1, 1)):

        def add(slot, value, qhalf=qhalf):
            dq_acc[qhalf, slot] += value

        grads.pair(qhalf, khalf, add)
    grads.write(dkv_out)
    for slot, out in ((0, keep_out), (1, send_out)):
        for peer in range(X):
            for b in range(2):
                for h in range(2):
                    r = peer * TOK + h * HALF
                    out[peer, b * HALF : (b + 1) * HALF, h * HEAD : (h + 1) * HEAD] = dq_acc[b, slot, r : r + HALF, :]


def merge_kernel(own_ref, got_ref, out_ref):
    out_ref[...] = (own_ref[...] + got_ref[...]).astype(BF16)


def dq_add_kernel(keep_ref, got_ref, *out_refs):
    part = lax.axis_index("x")
    for shift in range(X):
        to = (part + shift) % X
        out_refs[shift][...] = keep_ref[to] + got_ref[to]


def dq_sum_kernel(*refs):
    *in_refs, out_ref = refs
    total = in_refs[0][...]
    for ref in in_refs[1:]:
        total += ref[...]
    out_ref[...] = total.astype(BF16)


def dkv_sum_kernel(in_ref, out_ref):
    total = in_ref[0].astype(F32)
    for peer in range(1, Z):
        total += in_ref[peer].astype(F32)
    rows = total.astype(BF16)
    for peer in range(YH * X):
        out_ref[peer] = rows


def unpack_kernel(in_ref, dk_ref, dv_ref):
    for g in range(YH):
        for x in range(X):
            for b in range(2):
                at = b * HALF + x * SHARE
                dk_ref[g, at : at + SHARE, :] = in_ref[g * X + x, b * SHARE : (b + 1) * SHARE, :]
                dv_ref[g, at : at + SHARE, :] = in_ref[g * X + x, (2 + b) * SHARE : (3 + b) * SHARE, :]


def call(kernel, outs, n_in, scratch=(), flops=0, moved=1 << 20, vmem=8):
    shapes = tuple(jax.ShapeDtypeStruct(s, d) for s, d in outs)
    single = len(shapes) == 1
    return pl.pallas_call(
        kernel,
        out_shape=shapes[0] if single else shapes,
        in_specs=[VMEM_SPEC] * n_in,
        out_specs=VMEM_SPEC if single else (VMEM_SPEC,) * len(shapes),
        scratch_shapes=list(scratch),
        compiler_params=pltpu.CompilerParams(vmem_limit_bytes=vmem << 20),
        cost_estimate=pl.CostEstimate(flops=flops, bytes_accessed=moved, transcendentals=0),
    )


def exchange(value, axes):
    return lax.all_to_all(value, axes, 0, 0, tiled=True)


def shifted(value, axis, size, shift):
    return lax.ppermute(value, axis, [(i, (i + shift) % size) for i in range(size)])


def local(queries, key_codes, key_scale, value_codes, value_scale, evict_flags, out_forward, grad_output, log_norm):
    kmsg = call(prep_keys_kernel, [((Z, KMSG, HEAD), BF16)], 5, vmem=56)(
        key_codes, key_scale, value_codes, value_scale, evict_flags
    )
    kown = exchange(kmsg, "z")
    qmsg = call(prep_queries_kernel, [((QMSG, HEAD), BF16)], 4, vmem=56)(queries, grad_output, out_forward, log_norm)
    qmine = lax.all_gather(qmsg, "x", axis=0)
    kother = shifted(kown, "yl", YL, 1)
    qpeer = shifted(qmine, "core", CORE, 1)
    work = 5 * 2 * TILE * QHALF * HEAD
    acc = pltpu.VMEM((2, TILE, HEAD), F32)
    dq_acc = ((2, CORE, QSLOT, HEAD), F32)
    dkv_shape = ((Z, KROWS, HEAD), F32)
    piece = ((X, TOK, 2 * HEAD), F32)
    dkv_other, dq = call(
        other_kernel, [dkv_shape, dq_acc], 3, scratch=[acc, acc], flops=2 * work, vmem=24
    )(kother, qmine, qpeer)
    dkv_got = shifted(dkv_other, "yl", YL, 1)
    dkv_own, keep, send = call(
        own_kernel, [dkv_shape, piece, piece], 4, scratch=[acc, acc, pltpu.VMEM(*dq_acc)], flops=3 * work, vmem=24
    )(kown, qmine, qpeer, dq)
    got = shifted(send, "core", CORE, 1)
    parts = call(dq_add_kernel, [((TOK, 2 * HEAD), F32)] * X, 2)(keep, got)
    dkv = call(merge_kernel, [((Z, KROWS, HEAD), BF16)], 2)(dkv_own, dkv_got)
    dkv = exchange(dkv, "z")
    home = [parts[0]]
    for k in range(1, X):
        home.append(shifted(parts[k], "x", X, k))
    grad_queries = call(dq_sum_kernel, [((TOK, 2 * HEAD), BF16)], X)(*home)
    final = call(dkv_sum_kernel, [((YH * X, KROWS, HEAD), BF16)], 1)(dkv)
    every = exchange(final, ("yh", "x"))
    grad_keys, grad_values = call(unpack_kernel, [((2, TOK, HEAD), BF16)] * 2, 1)(every)
    return grad_queries, grad_keys, grad_values


def solution(mesh):
    fine = Mesh(mesh.devices.reshape(YL, Z, CORE, YH, X), ("yl", "z", "core", "yh", "x"))
    ctx, head = ("yl", "z", "core"), ("yh", "x")
    in_specs = (
        P(ctx, head),
        P(None, ctx, None),
        P(None, ctx),
        P(None, ctx, None),
        P(None, ctx),
        P(None, ctx),
        P(ctx, head),
        P(ctx, head),
        P(head, ctx),
    )
    out_specs = (P(ctx, head), P(None, ctx, None), P(None, ctx, None))
    return jax.shard_map(local, mesh=fine, in_specs=in_specs, out_specs=out_specs, check_vma=False)
```

```python
import math

import jax
import jax.numpy as jnp
from jax import lax
from jax.experimental import pallas as pl
from jax.experimental.pallas import tpu as pltpu
from jax.sharding import Mesh
from jax.sharding import PartitionSpec as P


DELAY = 256
HEAD = 128
TOK = 128
HALF = TOK // 2
YL, Z, CORE, YH, X = 2, 16, 2, 2, 4
CHIPS = YL * Z
SHARE = HALF // X
PEERS = CORE * X
BLOCKS = 2 * CHIPS * CORE
QROWS = 512
STAT = QROWS
QMSG = QROWS + 16
KROWS = 4 * SHARE
KMSG = KROWS + 8
TILE_SRC = CHIPS // 2
TILE = TILE_SRC * SHARE
QHALF = PEERS * TOK
QSLOT = X * TOK
SCALE = HEAD**-0.5
LOG2E = math.log2(math.e)
F32 = jnp.float32
BF16 = jnp.bfloat16
VMEM_SPEC = pl.BlockSpec(memory_space=pltpu.VMEM)


def split3(value):
    first = value.astype(BF16)
    rest = value - first.astype(F32)
    second = rest.astype(BF16)
    third = (rest - second.astype(F32)).astype(BF16)
    return [first, second, third]


def prep_keys_kernel(kc_ref, ks_ref, vc_ref, vs_ref, ev_ref, kmsg_ref):
    group = lax.axis_index("yh")
    part = lax.axis_index("x")

    def dequantized(code_ref, scale_ref, start):
        codes = code_ref[group, pl.ds(start, SHARE), :].astype(F32)
        scales = scale_ref[pl.ds(group, 1), :]
        lane = lax.broadcasted_iota(jnp.int32, (SHARE, TOK), 1)
        row = lax.broadcasted_iota(jnp.int32, (SHARE, TOK), 0) + start
        column = jnp.sum(jnp.where(lane == row, scales, 0.0), axis=1, keepdims=True)
        return (codes * column).astype(BF16)

    low = pl.multiple_of(part * SHARE, SHARE)
    high = pl.multiple_of(HALF + part * SHARE, SHARE)
    flags = jnp.broadcast_to(ev_ref[pl.ds(group, 1), :], (8, TOK)).astype(F32).astype(BF16)
    rows = jnp.concatenate(
        [
            dequantized(kc_ref, ks_ref, low),
            dequantized(kc_ref, ks_ref, high),
            dequantized(vc_ref, vs_ref, low),
            dequantized(vc_ref, vs_ref, high),
        ],
        axis=0,
    )
    for peer in range(Z):
        kmsg_ref[peer, 0:KROWS, :] = rows
        kmsg_ref[peer, KROWS:KMSG, :] = flags


def prep_queries_kernel(q_ref, do_ref, out_ref, norm_ref, qmsg_ref):
    q = q_ref[...]
    do = do_ref[...]
    product = do.astype(F32) * out_ref[...].astype(F32)
    norm = norm_ref[...] * LOG2E
    delta = jnp.concatenate(
        [jnp.sum(product[:, h * HEAD : (h + 1) * HEAD].T, axis=0, keepdims=True) for h in range(2)], axis=0
    )

    def halves(stat):
        return [
            jnp.concatenate([stat[0:1, b * HALF : (b + 1) * HALF], stat[1:2, b * HALF : (b + 1) * HALF]], axis=1)
            for b in range(2)
        ]

    norm_half, delta_half = halves(norm), halves(delta)
    stats = []
    for b in range(2):
        stats += split3(norm_half[b]) + split3(delta_half[b])
    stats = [s.astype(F32) for s in stats] + [jnp.zeros((4, TOK), F32)]
    stats = jnp.concatenate(stats, axis=0).astype(BF16)

    def reordered(value):
        return jnp.concatenate(
            [value[b * HALF : (b + 1) * HALF, h * HEAD : (h + 1) * HEAD] for b in range(2) for h in range(2)],
            axis=0,
        )

    qmsg_ref[0:256, :] = reordered(q)
    qmsg_ref[256:512, :] = reordered(do)
    qmsg_ref[QROWS:QMSG, :] = stats


class Grads:
    def __init__(self, kmsg_refs, qmsg_ref, other, dk_acc, dv_acc, dq_acc):
        self.kmsg_refs, self.qmsg_ref = kmsg_refs, qmsg_ref
        self.dk_acc, self.dv_acc, self.dq_acc = dk_acc, dv_acc, dq_acc
        self.core = lax.axis_index("core")
        self.part = lax.axis_index("x")
        self.column = lax.axis_index("yl")
        self.chip = (1 - self.column if other else self.column) * Z + lax.axis_index("z")

    def keys(self, slot, khalf):
        kmsg_ref = self.kmsg_refs[slot]
        core = self.core if slot == 0 else 1 - self.core
        index = lax.broadcasted_iota(jnp.int32, (TILE, 1), 0)
        src = self.column * Z + index // SHARE
        block = jnp.where(khalf == 0, CORE * src + core, BLOCKS - 1 - CORE * src - core)
        offset = self.part * SHARE + index % SHARE
        pos = block * HALF + offset
        flags = kmsg_ref[:, KROWS : KROWS + 8, :][:, 0, :].astype(F32)
        wide = jnp.broadcast_to(flags[:, None, :], (Z, SHARE, TOK)).reshape(TILE, TOK)
        lane = lax.broadcasted_iota(jnp.int32, (TILE, TOK), 1)
        flag = jnp.sum(jnp.where(lane == khalf * HALF + offset, wide, 0.0), axis=1, keepdims=True)
        last = jnp.where(flag > 0.5, pos + DELAY - 1, BLOCKS * HALF)
        krow = pl.multiple_of(khalf * SHARE, SHARE)
        vrow = pl.multiple_of((2 + khalf) * SHARE, SHARE)
        k = kmsg_ref[:, pl.ds(krow, SHARE), :].reshape(TILE, HEAD)
        v = kmsg_ref[:, pl.ds(vrow, SHARE), :].reshape(TILE, HEAD)
        return k, v, pos, last

    def stat_row(self, qmsg_ref, qhalf, which):
        rows = []
        for peer in range(X):
            both = qmsg_ref[peer, STAT : STAT + 16, :].astype(F32)

            def total(b):
                at = b * 6 + which * 3
                return both[at : at + 1] + both[at + 1 : at + 2] + both[at + 2 : at + 3]

            rows.append(jnp.where(qhalf == 0, total(0), total(1)))
        return jnp.concatenate(rows, axis=1)

    def pair(self, qhalf, khalf):
        q0 = pl.multiple_of(qhalf * TOK, TOK)
        d0 = pl.multiple_of((2 + qhalf) * TOK, TOK)
        norm = self.stat_row(self.qmsg_ref, qhalf, 0)
        delta = self.stat_row(self.qmsg_ref, qhalf, 1)
        qblock = jnp.where(qhalf == 0, CORE * self.chip + self.core, BLOCKS - 1 - CORE * self.chip - self.core)
        qpos = qblock * HALF + lax.broadcasted_iota(jnp.int32, (1, QSLOT), 1) % HALF
        q = self.qmsg_ref[:, pl.ds(q0, TOK), :].reshape(QSLOT, HEAD)
        do = self.qmsg_ref[:, pl.ds(d0, TOK), :].reshape(QSLOT, HEAD)
        for slot in range(CORE):
            k, v, kpos, klast = self.keys(slot, khalf)
            s = lax.dot_general(k, q, (((1,), (1,)), ((), ())), preferred_element_type=F32)
            dp = lax.dot_general(v, do, (((1,), (1,)), ((), ())), preferred_element_type=F32)
            seen = (kpos <= qpos) & (qpos <= klast)
            w = jnp.where(seen, jnp.exp2(s * (SCALE * LOG2E) - norm), 0.0)
            ds = ((w * SCALE) * (dp - delta)).astype(BF16)
            wb = w.astype(BF16)
            self.dv_acc[slot, khalf] += jnp.dot(wb, do, preferred_element_type=F32)
            self.dk_acc[slot, khalf] += jnp.dot(ds, q, preferred_element_type=F32)
            self.dq_acc[qhalf] += lax.dot_general(ds, k, (((0,), (0,)), ((), ())), preferred_element_type=F32)

    def write_keys(self, slot, out_ref):
        for khalf in range(2):
            dk = self.dk_acc[slot, khalf].reshape(Z, SHARE, HEAD)
            dv = self.dv_acc[slot, khalf].reshape(Z, SHARE, HEAD)
            out_ref[:, khalf * SHARE : (khalf + 1) * SHARE, :] = dk
            out_ref[:, (2 + khalf) * SHARE : (3 + khalf) * SHARE, :] = dv

    def write_queries(self, out_ref):
        for peer in range(X):
            for b in range(2):
                for h in range(2):
                    r = peer * TOK + h * HALF
                    value = self.dq_acc[b, r : r + HALF, :]
                    out_ref[peer, b * HALF : (b + 1) * HALF, h * HEAD : (h + 1) * HEAD] = value


def own_kernel(kown_ref, kpeer_ref, qown_ref, dk_out, dv_out, dq_out, dq_acc):
    grads = Grads((kown_ref, kpeer_ref), qown_ref, False, dk_out, dv_out, dq_acc)
    dk_out[...] = jnp.zeros_like(dk_out)
    dv_out[...] = jnp.zeros_like(dv_out)
    dq_acc[...] = jnp.zeros_like(dq_acc)
    for qhalf, khalf in ((0, 0), (1, 0), (1, 1)):
        grads.pair(qhalf, khalf)
    grads.write_queries(dq_out)


def other_kernel(
    kown_ref, kpeer_ref, qother_ref, dk_ref, dv_ref, mine_out, theirs_out, dq_out, dk_acc, dv_acc, dq_acc
):
    grads = Grads((kown_ref, kpeer_ref), qother_ref, True, dk_acc, dv_acc, dq_acc)
    dk_acc[...] = dk_ref[...]
    dv_acc[...] = dv_ref[...]
    dq_acc[...] = jnp.zeros_like(dq_acc)
    column = lax.axis_index("yl")
    for qhalf, khalf in ((1, 0), (column, column)):
        grads.pair(qhalf, khalf)
    grads.write_keys(0, mine_out)
    grads.write_keys(1, theirs_out)
    grads.write_queries(dq_out)


def merge_kernel(own_ref, got_ref, out_ref):
    out_ref[...] = (own_ref[...] + got_ref[...]).astype(BF16)


def dq_add_kernel(keep_ref, got_ref, *out_refs):
    part = lax.axis_index("x")
    for shift in range(X):
        to = (part + shift) % X
        out_refs[shift][...] = keep_ref[to] + got_ref[to]


def dq_sum_kernel(*refs):
    *in_refs, out_ref = refs
    total = in_refs[0][...]
    for ref in in_refs[1:]:
        total += ref[...]
    out_ref[...] = total.astype(BF16)


def dkv_sum_kernel(in_ref, out_ref):
    total = in_ref[0].astype(F32)
    for peer in range(1, Z):
        total += in_ref[peer].astype(F32)
    rows = total.astype(BF16)
    for peer in range(YH * X):
        out_ref[peer] = rows


def unpack_kernel(in_ref, dk_ref, dv_ref):
    for g in range(YH):
        for x in range(X):
            for b in range(2):
                at = b * HALF + x * SHARE
                dk_ref[g, at : at + SHARE, :] = in_ref[g * X + x, b * SHARE : (b + 1) * SHARE, :]
                dv_ref[g, at : at + SHARE, :] = in_ref[g * X + x, (2 + b) * SHARE : (3 + b) * SHARE, :]


def call(kernel, outs, n_in, scratch=(), flops=0, moved=1 << 20, vmem=8):
    shapes = tuple(jax.ShapeDtypeStruct(s, d) for s, d in outs)
    single = len(shapes) == 1
    return pl.pallas_call(
        kernel,
        out_shape=shapes[0] if single else shapes,
        in_specs=[VMEM_SPEC] * n_in,
        out_specs=VMEM_SPEC if single else (VMEM_SPEC,) * len(shapes),
        scratch_shapes=list(scratch),
        compiler_params=pltpu.CompilerParams(vmem_limit_bytes=vmem << 20),
        cost_estimate=pl.CostEstimate(flops=flops, bytes_accessed=moved, transcendentals=0),
    )


def exchange(value, axes):
    return lax.all_to_all(value, axes, 0, 0, tiled=True)


def shifted(value, axis, size, shift):
    return lax.ppermute(value, axis, [(i, (i + shift) % size) for i in range(size)])


def local(queries, key_codes, key_scale, value_codes, value_scale, evict_flags, out_forward, grad_output, log_norm):
    kmsg = call(prep_keys_kernel, [((Z, KMSG, HEAD), BF16)], 5, vmem=56)(
        key_codes, key_scale, value_codes, value_scale, evict_flags
    )
    kown = exchange(kmsg, "z")
    qmsg = call(prep_queries_kernel, [((QMSG, HEAD), BF16)], 4, vmem=56)(queries, grad_output, out_forward, log_norm)
    qmine = lax.all_gather(qmsg, "x", axis=0)
    qother = shifted(qmine, "yl", YL, 1)
    kpeer = shifted(kown, "core", CORE, 1)
    work = 5 * 2 * TILE * QHALF * HEAD
    acc = ((CORE, 2, TILE, HEAD), F32)
    dq_acc = pltpu.VMEM((2, QSLOT, HEAD), F32)
    dkv_shape = ((Z, KROWS, HEAD), F32)
    piece = ((X, TOK, 2 * HEAD), F32)
    dk, dv, keep = call(own_kernel, [acc, acc, piece], 3, scratch=[dq_acc], flops=3 * work, vmem=24)(kown, kpeer, qmine)
    mine, theirs, send = call(
        other_kernel,
        [dkv_shape, dkv_shape, piece],
        5,
        scratch=[pltpu.VMEM(*acc), pltpu.VMEM(*acc), dq_acc],
        flops=2 * work,
        vmem=24,
    )(kown, kpeer, qother, dk, dv)
    dkv_got = shifted(theirs, "core", CORE, 1)
    got = shifted(send, "yl", YL, 1)
    parts = call(dq_add_kernel, [((TOK, 2 * HEAD), F32)] * X, 2)(keep, got)
    dkv = call(merge_kernel, [((Z, KROWS, HEAD), BF16)], 2)(mine, dkv_got)
    dkv = exchange(dkv, "z")
    home = [parts[0]]
    for k in range(1, X):
        home.append(shifted(parts[k], "x", X, k))
    grad_queries = call(dq_sum_kernel, [((TOK, 2 * HEAD), BF16)], X)(*home)
    final = call(dkv_sum_kernel, [((YH * X, KROWS, HEAD), BF16)], 1)(dkv)
    every = exchange(final, ("yh", "x"))
    grad_keys, grad_values = call(unpack_kernel, [((2, TOK, HEAD), BF16)] * 2, 1)(every)
    return grad_queries, grad_keys, grad_values


def solution(mesh):
    fine = Mesh(mesh.devices.reshape(YL, Z, CORE, YH, X), ("yl", "z", "core", "yh", "x"))
    ctx, head = ("yl", "z", "core"), ("yh", "x")
    in_specs = (
        P(ctx, head),
        P(None, ctx, None),
        P(None, ctx),
        P(None, ctx, None),
        P(None, ctx),
        P(None, ctx),
        P(ctx, head),
        P(ctx, head),
        P(head, ctx),
    )
    out_specs = (P(ctx, head), P(None, ctx, None), P(None, ctx, None))
    return jax.shard_map(local, mesh=fine, in_specs=in_specs, out_specs=out_specs, check_vma=False)
```

```python
import math

import jax
import jax.numpy as jnp
from jax import lax
from jax.experimental import pallas as pl
from jax.experimental.pallas import tpu as pltpu
from jax.sharding import Mesh
from jax.sharding import PartitionSpec as P


DELAY = 256
HEAD = 128
TOK = 128
HALF = TOK // 2
YL, Z, CORE, YH, X = 2, 16, 2, 2, 4
CHIPS = YL * Z
SHARE = HALF // X
PEERS = CORE * X
BLOCKS = 2 * CHIPS * CORE
QROWS = 512
STAT = QROWS
QMSG = QROWS + 16
KROWS = 4 * SHARE
KMSG = KROWS + 8
TILE_SRC = CHIPS // 2
TILE = TILE_SRC * SHARE
QHALF = PEERS * TOK
QSLOT = X * TOK
SCALE = HEAD**-0.5
LOG2E = math.log2(math.e)
F32 = jnp.float32
BF16 = jnp.bfloat16
VMEM_SPEC = pl.BlockSpec(memory_space=pltpu.VMEM)


def split3(value):
    first = value.astype(BF16)
    rest = value - first.astype(F32)
    second = rest.astype(BF16)
    third = (rest - second.astype(F32)).astype(BF16)
    return [first, second, third]


def prep_keys(kc_ref, ks_ref, vc_ref, vs_ref, ev_ref, kmsg_ref):
    group = lax.axis_index("yh")
    part = lax.axis_index("x")

    def dequantized(code_ref, scale_ref, start):
        codes = code_ref[group, pl.ds(start, SHARE), :].astype(F32)
        scales = scale_ref[pl.ds(group, 1), :]
        lane = lax.broadcasted_iota(jnp.int32, (SHARE, TOK), 1)
        row = lax.broadcasted_iota(jnp.int32, (SHARE, TOK), 0) + start
        column = jnp.sum(jnp.where(lane == row, scales, 0.0), axis=1, keepdims=True)
        return (codes * column).astype(BF16)

    low = pl.multiple_of(part * SHARE, SHARE)
    high = pl.multiple_of(HALF + part * SHARE, SHARE)
    flags = jnp.broadcast_to(ev_ref[pl.ds(group, 1), :], (8, TOK)).astype(F32).astype(BF16)
    rows = jnp.concatenate(
        [
            dequantized(kc_ref, ks_ref, low),
            dequantized(kc_ref, ks_ref, high),
            dequantized(vc_ref, vs_ref, low),
            dequantized(vc_ref, vs_ref, high),
        ],
        axis=0,
    )
    for peer in range(Z):
        kmsg_ref[peer, 0:KROWS, :] = rows
        kmsg_ref[peer, KROWS:KMSG, :] = flags


def prep_queries(q_ref, do_ref, out_ref, norm_ref, qmsg_ref):
    q = q_ref[...]
    do = do_ref[...]
    product = do.astype(F32) * out_ref[...].astype(F32)
    norm = norm_ref[...] * LOG2E
    delta = jnp.concatenate(
        [jnp.sum(product[:, h * HEAD : (h + 1) * HEAD].T, axis=0, keepdims=True) for h in range(2)], axis=0
    )

    def halves(stat):
        return [
            jnp.concatenate([stat[0:1, b * HALF : (b + 1) * HALF], stat[1:2, b * HALF : (b + 1) * HALF]], axis=1)
            for b in range(2)
        ]

    norm_half, delta_half = halves(norm), halves(delta)
    stats = []
    for b in range(2):
        stats += split3(norm_half[b]) + split3(delta_half[b])
    stats = [s.astype(F32) for s in stats] + [jnp.zeros((4, TOK), F32)]
    stats = jnp.concatenate(stats, axis=0).astype(BF16)

    def reordered(value):
        return jnp.concatenate(
            [value[b * HALF : (b + 1) * HALF, h * HEAD : (h + 1) * HEAD] for b in range(2) for h in range(2)],
            axis=0,
        )

    qmsg_ref[0:256, :] = reordered(q)
    qmsg_ref[256:512, :] = reordered(do)
    qmsg_ref[QROWS:QMSG, :] = stats


def prep_kernel(
    kc_ref, ks_ref, vc_ref, vs_ref, ev_ref, q_ref, do_ref, out_ref, norm_ref, kmsg_ref, qmsg_ref
):
    prep_keys(kc_ref, ks_ref, vc_ref, vs_ref, ev_ref, kmsg_ref)
    prep_queries(q_ref, do_ref, out_ref, norm_ref, qmsg_ref)


class Grads:
    def __init__(self, kmsg_refs, qmsg_ref, other, dk_acc, dv_acc, dq_acc):
        self.kmsg_refs, self.qmsg_ref = kmsg_refs, qmsg_ref
        self.dk_acc, self.dv_acc, self.dq_acc = dk_acc, dv_acc, dq_acc
        self.core = lax.axis_index("core")
        self.part = lax.axis_index("x")
        self.column = lax.axis_index("yl")
        self.chip = (1 - self.column if other else self.column) * Z + lax.axis_index("z")

    def keys(self, slot, khalf):
        kmsg_ref = self.kmsg_refs[slot]
        core = self.core if slot == 0 else 1 - self.core
        index = lax.broadcasted_iota(jnp.int32, (TILE, 1), 0)
        src = self.column * Z + index // SHARE
        block = jnp.where(khalf == 0, CORE * src + core, BLOCKS - 1 - CORE * src - core)
        offset = self.part * SHARE + index % SHARE
        pos = block * HALF + offset
        flags = kmsg_ref[:, KROWS : KROWS + 8, :][:, 0, :].astype(F32)
        wide = jnp.broadcast_to(flags[:, None, :], (Z, SHARE, TOK)).reshape(TILE, TOK)
        lane = lax.broadcasted_iota(jnp.int32, (TILE, TOK), 1)
        flag = jnp.sum(jnp.where(lane == khalf * HALF + offset, wide, 0.0), axis=1, keepdims=True)
        last = jnp.where(flag > 0.5, pos + DELAY - 1, BLOCKS * HALF)
        krow = pl.multiple_of(khalf * SHARE, SHARE)
        vrow = pl.multiple_of((2 + khalf) * SHARE, SHARE)
        k = kmsg_ref[:, pl.ds(krow, SHARE), :].reshape(TILE, HEAD)
        v = kmsg_ref[:, pl.ds(vrow, SHARE), :].reshape(TILE, HEAD)
        return k, v, pos, last

    def stat_row(self, qmsg_ref, qhalf, which):
        rows = []
        for peer in range(X):
            both = qmsg_ref[peer, STAT : STAT + 16, :].astype(F32)

            def total(b):
                at = b * 6 + which * 3
                return both[at : at + 1] + both[at + 1 : at + 2] + both[at + 2 : at + 3]

            rows.append(jnp.where(qhalf == 0, total(0), total(1)))
        return jnp.concatenate(rows, axis=1)

    def pair(self, qhalf, khalf):
        q0 = pl.multiple_of(qhalf * TOK, TOK)
        d0 = pl.multiple_of((2 + qhalf) * TOK, TOK)
        norm = self.stat_row(self.qmsg_ref, qhalf, 0)
        delta = self.stat_row(self.qmsg_ref, qhalf, 1)
        qblock = jnp.where(qhalf == 0, CORE * self.chip + self.core, BLOCKS - 1 - CORE * self.chip - self.core)
        qpos = qblock * HALF + lax.broadcasted_iota(jnp.int32, (1, QSLOT), 1) % HALF
        q = self.qmsg_ref[:, pl.ds(q0, TOK), :].reshape(QSLOT, HEAD)
        do = self.qmsg_ref[:, pl.ds(d0, TOK), :].reshape(QSLOT, HEAD)
        for slot in range(CORE):
            k, v, kpos, klast = self.keys(slot, khalf)
            s = lax.dot_general(k, q, (((1,), (1,)), ((), ())), preferred_element_type=F32)
            dp = lax.dot_general(v, do, (((1,), (1,)), ((), ())), preferred_element_type=F32)
            seen = (kpos <= qpos) & (qpos <= klast)
            w = jnp.where(seen, jnp.exp2(s * (SCALE * LOG2E) - norm), 0.0)
            ds = ((w * SCALE) * (dp - delta)).astype(BF16)
            wb = w.astype(BF16)
            self.dv_acc[slot, khalf] += jnp.dot(wb, do, preferred_element_type=F32)
            self.dk_acc[slot, khalf] += jnp.dot(ds, q, preferred_element_type=F32)
            self.dq_acc[qhalf] += lax.dot_general(ds, k, (((0,), (0,)), ((), ())), preferred_element_type=F32)

    def write_keys(self, slot, out_ref):
        for khalf in range(2):
            dk = self.dk_acc[slot, khalf].reshape(Z, SHARE, HEAD)
            dv = self.dv_acc[slot, khalf].reshape(Z, SHARE, HEAD)
            out_ref[:, khalf * SHARE : (khalf + 1) * SHARE, :] = dk
            out_ref[:, (2 + khalf) * SHARE : (3 + khalf) * SHARE, :] = dv

    def write_queries(self, out_ref):
        for peer in range(X):
            for b in range(2):
                for h in range(2):
                    r = peer * TOK + h * HALF
                    value = self.dq_acc[b, r : r + HALF, :]
                    out_ref[peer, b * HALF : (b + 1) * HALF, h * HEAD : (h + 1) * HEAD] = value.astype(out_ref.dtype)


def own_kernel(kown_ref, kpeer_ref, qown_ref, dk_out, dv_out, dq_out, dq_acc):
    grads = Grads((kown_ref, kpeer_ref), qown_ref, False, dk_out, dv_out, dq_acc)
    dk_out[...] = jnp.zeros_like(dk_out)
    dv_out[...] = jnp.zeros_like(dv_out)
    dq_acc[...] = jnp.zeros_like(dq_acc)
    for qhalf, khalf in ((0, 0), (1, 0), (1, 1)):
        grads.pair(qhalf, khalf)
    grads.write_queries(dq_out)


def other_kernel(
    kown_ref, kpeer_ref, qother_ref, dk_ref, dv_ref, mine_out, theirs_out, dq_out, dk_acc, dv_acc, dq_acc
):
    grads = Grads((kown_ref, kpeer_ref), qother_ref, True, dk_acc, dv_acc, dq_acc)
    dk_acc[...] = dk_ref[...]
    dv_acc[...] = dv_ref[...]
    dq_acc[...] = jnp.zeros_like(dq_acc)
    column = lax.axis_index("yl")
    for qhalf, khalf in ((1, 0), (column, column)):
        grads.pair(qhalf, khalf)
    grads.write_keys(0, mine_out)
    grads.write_keys(1, theirs_out)
    grads.write_queries(dq_out)


def merge_kernel(own_ref, got_ref, out_ref):
    out_ref[...] = (own_ref[...] + got_ref[...]).astype(BF16)


def dq_add_kernel(keep_ref, got_ref, keep_out, send_out):
    upper = lax.axis_index("x") // 2
    for j in range(2):
        mine = upper * 2 + j
        theirs = (1 - upper) * 2 + j
        keep_out[j] = keep_ref[mine] + got_ref[mine].astype(F32)
        send_out[j] = keep_ref[theirs] + got_ref[theirs].astype(F32)


def dq_half_kernel(keep_ref, got_ref, keep_out, send_out):
    odd = lax.axis_index("x") % 2
    keep_out[...] = keep_ref[odd] + got_ref[odd]
    send_out[...] = keep_ref[1 - odd] + got_ref[1 - odd]


def dq_sum_kernel(keep_ref, got_ref, out_ref):
    out_ref[...] = (keep_ref[...] + got_ref[...]).astype(BF16)


def dkv_sum_kernel(in_ref, out_ref):
    total = in_ref[0].astype(F32)
    for peer in range(1, Z):
        total += in_ref[peer].astype(F32)
    rows = total.astype(BF16)
    for peer in range(YH * X):
        out_ref[peer] = rows


def unpack_kernel(in_ref, dk_ref, dv_ref):
    for g in range(YH):
        for x in range(X):
            for b in range(2):
                at = b * HALF + x * SHARE
                dk_ref[g, at : at + SHARE, :] = in_ref[g * X + x, b * SHARE : (b + 1) * SHARE, :]
                dv_ref[g, at : at + SHARE, :] = in_ref[g * X + x, (2 + b) * SHARE : (3 + b) * SHARE, :]


def call(kernel, outs, n_in, scratch=(), flops=0, moved=1 << 20, vmem=8):
    shapes = tuple(jax.ShapeDtypeStruct(s, d) for s, d in outs)
    single = len(shapes) == 1
    return pl.pallas_call(
        kernel,
        out_shape=shapes[0] if single else shapes,
        in_specs=[VMEM_SPEC] * n_in,
        out_specs=VMEM_SPEC if single else (VMEM_SPEC,) * len(shapes),
        scratch_shapes=list(scratch),
        compiler_params=pltpu.CompilerParams(vmem_limit_bytes=vmem << 20),
        cost_estimate=pl.CostEstimate(flops=flops, bytes_accessed=moved, transcendentals=0),
    )


def exchange(value, axes):
    return lax.all_to_all(value, axes, 0, 0, tiled=True)


def shifted(value, axis, size, shift):
    return lax.ppermute(value, axis, [(i, (i + shift) % size) for i in range(size)])


def local(queries, key_codes, key_scale, value_codes, value_scale, evict_flags, out_forward, grad_output, log_norm):
    kmsg, qmsg = call(prep_kernel, [((Z, KMSG, HEAD), BF16), ((QMSG, HEAD), BF16)], 9, vmem=56)(
        key_codes,
        key_scale,
        value_codes,
        value_scale,
        evict_flags,
        queries,
        grad_output,
        out_forward,
        log_norm,
    )
    kown = exchange(kmsg, "z")
    qmine = lax.all_gather(qmsg, "x", axis=0)
    qother = shifted(qmine, "yl", YL, 1)
    kpeer = shifted(kown, "core", CORE, 1)
    work = 5 * 2 * TILE * QHALF * HEAD
    acc = ((CORE, 2, TILE, HEAD), F32)
    dq_acc = pltpu.VMEM((2, QSLOT, HEAD), F32)
    dkv_shape = ((Z, KROWS, HEAD), F32)
    piece = ((X, TOK, 2 * HEAD), F32)
    dk, dv, keep = call(own_kernel, [acc, acc, piece], 3, scratch=[dq_acc], flops=3 * work, vmem=24)(kown, kpeer, qmine)
    mine, theirs, send = call(
        other_kernel,
        [dkv_shape, dkv_shape, (piece[0], BF16)],
        5,
        scratch=[pltpu.VMEM(*acc), pltpu.VMEM(*acc), dq_acc],
        flops=2 * work,
        vmem=24,
    )(kown, kpeer, qother, dk, dv)
    dkv_got = shifted(theirs, "core", CORE, 1)
    got = shifted(send, "yl", YL, 1)
    dkv = call(merge_kernel, [((Z, KROWS, HEAD), BF16)], 2)(mine, dkv_got)
    dkv = exchange(dkv, "z")
    two = ((2, TOK, 2 * HEAD), F32)
    one = ((TOK, 2 * HEAD), F32)
    keep, send = call(dq_add_kernel, [two, two], 2)(keep, got)
    got = lax.ppermute(send, "x", [(i, i ^ 2) for i in range(X)])
    keep, send = call(dq_half_kernel, [one, one], 2)(keep, got)
    got = lax.ppermute(send, "x", [(i, i ^ 1) for i in range(X)])
    grad_queries = call(dq_sum_kernel, [((TOK, 2 * HEAD), BF16)], 2)(keep, got)
    final = call(dkv_sum_kernel, [((YH * X, KROWS, HEAD), BF16)], 1)(dkv)
    every = exchange(final, ("yh", "x"))
    grad_keys, grad_values = call(unpack_kernel, [((2, TOK, HEAD), BF16)] * 2, 1)(every)
    return grad_queries, grad_keys, grad_values


def solution(mesh):
    fine = Mesh(mesh.devices.reshape(YL, Z, CORE, YH, X), ("yl", "z", "core", "yh", "x"))
    ctx, head = ("yl", "z", "core"), ("yh", "x")
    in_specs = (
        P(ctx, head),
        P(None, ctx, None),
        P(None, ctx),
        P(None, ctx, None),
        P(None, ctx),
        P(None, ctx),
        P(ctx, head),
        P(ctx, head),
        P(head, ctx),
    )
    out_specs = (P(ctx, head), P(None, ctx, None), P(None, ctx, None))
    return jax.shard_map(local, mesh=fine, in_specs=in_specs, out_specs=out_specs, check_vma=False)
```

```python
import math

import jax
import jax.numpy as jnp
from jax import lax
from jax.experimental import pallas as pl
from jax.experimental.pallas import tpu as pltpu
from jax.sharding import Mesh
from jax.sharding import PartitionSpec as P


DELAY = 256
HEAD = 128
TOK = 128
HALF = TOK // 2
YL, Z, CORE, YH, X = 2, 16, 2, 2, 4
CHIPS = YL * Z
SHARE = HALF // X
PEERS = CORE * X
BLOCKS = 2 * CHIPS * CORE
QROWS = 512
STAT = QROWS
QMSG = QROWS + 16
KROWS = 4 * SHARE
KMSG = KROWS + 8
TILE_SRC = CHIPS // 2
TILE = TILE_SRC * SHARE
QHALF = PEERS * TOK
QSLOT = X * TOK
SCALE = HEAD**-0.5
LOG2E = math.log2(math.e)
F32 = jnp.float32
BF16 = jnp.bfloat16
VMEM_SPEC = pl.BlockSpec(memory_space=pltpu.VMEM)


def split3(value):
    first = value.astype(BF16)
    rest = value - first.astype(F32)
    second = rest.astype(BF16)
    third = (rest - second.astype(F32)).astype(BF16)
    return [first, second, third]


def prep_keys(kc_ref, ks_ref, vc_ref, vs_ref, ev_ref, kmsg_ref):
    group = lax.axis_index("yh")
    part = lax.axis_index("x")

    def dequantized(code_ref, scale_ref, start):
        codes = code_ref[group, pl.ds(start, SHARE), :].astype(F32)
        scales = scale_ref[pl.ds(group, 1), :]
        lane = lax.broadcasted_iota(jnp.int32, (SHARE, TOK), 1)
        row = lax.broadcasted_iota(jnp.int32, (SHARE, TOK), 0) + start
        column = jnp.sum(jnp.where(lane == row, scales, 0.0), axis=1, keepdims=True)
        return (codes * column).astype(BF16)

    low = pl.multiple_of(part * SHARE, SHARE)
    high = pl.multiple_of(HALF + part * SHARE, SHARE)
    flags = jnp.broadcast_to(ev_ref[pl.ds(group, 1), :], (8, TOK)).astype(F32).astype(BF16)
    rows = jnp.concatenate(
        [
            dequantized(kc_ref, ks_ref, low),
            dequantized(kc_ref, ks_ref, high),
            dequantized(vc_ref, vs_ref, low),
            dequantized(vc_ref, vs_ref, high),
        ],
        axis=0,
    )
    for peer in range(Z):
        kmsg_ref[peer, 0:KROWS, :] = rows
        kmsg_ref[peer, KROWS:KMSG, :] = flags


def prep_queries(q_ref, do_ref, out_ref, norm_ref, qmsg_ref):
    q = q_ref[...]
    do = do_ref[...]
    product = do.astype(F32) * out_ref[...].astype(F32)
    norm = norm_ref[...] * LOG2E
    delta = jnp.concatenate(
        [jnp.sum(product[:, h * HEAD : (h + 1) * HEAD].T, axis=0, keepdims=True) for h in range(2)], axis=0
    )

    def halves(stat):
        return [
            jnp.concatenate([stat[0:1, b * HALF : (b + 1) * HALF], stat[1:2, b * HALF : (b + 1) * HALF]], axis=1)
            for b in range(2)
        ]

    norm_half, delta_half = halves(norm), halves(delta)
    stats = []
    for b in range(2):
        stats += split3(norm_half[b]) + split3(delta_half[b])
    stats = [s.astype(F32) for s in stats] + [jnp.zeros((4, TOK), F32)]
    stats = jnp.concatenate(stats, axis=0).astype(BF16)

    def reordered(value):
        return jnp.concatenate(
            [value[b * HALF : (b + 1) * HALF, h * HEAD : (h + 1) * HEAD] for b in range(2) for h in range(2)],
            axis=0,
        )

    qmsg_ref[0:256, :] = reordered(q)
    qmsg_ref[256:512, :] = reordered(do)
    qmsg_ref[QROWS:QMSG, :] = stats


def prep_kernel(
    kc_ref, ks_ref, vc_ref, vs_ref, ev_ref, q_ref, do_ref, out_ref, norm_ref, kmsg_ref, qmsg_ref
):
    prep_keys(kc_ref, ks_ref, vc_ref, vs_ref, ev_ref, kmsg_ref)
    prep_queries(q_ref, do_ref, out_ref, norm_ref, qmsg_ref)


class Grads:
    def __init__(self, kmsg_refs, qmsg_ref, other, dk_acc, dv_acc, dq_acc):
        self.kmsg_refs, self.qmsg_ref = kmsg_refs, qmsg_ref
        self.dk_acc, self.dv_acc, self.dq_acc = dk_acc, dv_acc, dq_acc
        self.core = lax.axis_index("core")
        self.part = lax.axis_index("x")
        self.column = lax.axis_index("yl")
        self.chip = (1 - self.column if other else self.column) * Z + lax.axis_index("z")

    def keys(self, slot, khalf):
        kmsg_ref = self.kmsg_refs[slot]
        core = self.core if slot == 0 else 1 - self.core
        index = lax.broadcasted_iota(jnp.int32, (TILE, 1), 0)
        src = self.column * Z + index // SHARE
        block = jnp.where(khalf == 0, CORE * src + core, BLOCKS - 1 - CORE * src - core)
        offset = self.part * SHARE + index % SHARE
        pos = block * HALF + offset
        flags = kmsg_ref[:, KROWS : KROWS + 8, :][:, 0, :].astype(F32)
        wide = jnp.broadcast_to(flags[:, None, :], (Z, SHARE, TOK)).reshape(TILE, TOK)
        lane = lax.broadcasted_iota(jnp.int32, (TILE, TOK), 1)
        flag = jnp.sum(jnp.where(lane == khalf * HALF + offset, wide, 0.0), axis=1, keepdims=True)
        last = jnp.where(flag > 0.5, pos + DELAY - 1, BLOCKS * HALF)
        krow = pl.multiple_of(khalf * SHARE, SHARE)
        vrow = pl.multiple_of((2 + khalf) * SHARE, SHARE)
        k = kmsg_ref[:, pl.ds(krow, SHARE), :].reshape(TILE, HEAD)
        v = kmsg_ref[:, pl.ds(vrow, SHARE), :].reshape(TILE, HEAD)
        return k, v, pos, last

    def stat_row(self, qmsg_ref, qhalf, which):
        rows = []
        for peer in range(X):
            both = qmsg_ref[peer, STAT : STAT + 16, :].astype(F32)

            def total(b):
                at = b * 6 + which * 3
                return both[at : at + 1] + both[at + 1 : at + 2] + both[at + 2 : at + 3]

            rows.append(jnp.where(qhalf == 0, total(0), total(1)))
        return jnp.concatenate(rows, axis=1)

    def pair(self, qhalf, khalf):
        q0 = pl.multiple_of(qhalf * TOK, TOK)
        d0 = pl.multiple_of((2 + qhalf) * TOK, TOK)
        norm = self.stat_row(self.qmsg_ref, qhalf, 0)
        delta = self.stat_row(self.qmsg_ref, qhalf, 1)
        qblock = jnp.where(qhalf == 0, CORE * self.chip + self.core, BLOCKS - 1 - CORE * self.chip - self.core)
        qpos = qblock * HALF + lax.broadcasted_iota(jnp.int32, (1, QSLOT), 1) % HALF
        q = self.qmsg_ref[:, pl.ds(q0, TOK), :].reshape(QSLOT, HEAD)
        do = self.qmsg_ref[:, pl.ds(d0, TOK), :].reshape(QSLOT, HEAD)
        for slot in range(CORE):
            k, v, kpos, klast = self.keys(slot, khalf)
            s = lax.dot_general(k, q, (((1,), (1,)), ((), ())), preferred_element_type=F32)
            dp = lax.dot_general(v, do, (((1,), (1,)), ((), ())), preferred_element_type=F32)
            seen = (kpos <= qpos) & (qpos <= klast)
            w = jnp.where(seen, jnp.exp2(s * (SCALE * LOG2E) - norm), 0.0)
            ds = ((w * SCALE) * (dp - delta)).astype(BF16)
            wb = w.astype(BF16)
            self.dv_acc[slot, khalf] += jnp.dot(wb, do, preferred_element_type=F32)
            self.dk_acc[slot, khalf] += jnp.dot(ds, q, preferred_element_type=F32)
            self.dq_acc[qhalf] += lax.dot_general(ds, k, (((0,), (0,)), ((), ())), preferred_element_type=F32)

    def write_keys(self, slot, out_ref):
        for khalf in range(2):
            dk = self.dk_acc[slot, khalf].reshape(Z, SHARE, HEAD)
            dv = self.dv_acc[slot, khalf].reshape(Z, SHARE, HEAD)
            out_ref[:, khalf * SHARE : (khalf + 1) * SHARE, :] = dk
            out_ref[:, (2 + khalf) * SHARE : (3 + khalf) * SHARE, :] = dv

    def write_queries(self, out_ref):
        for peer in range(X):
            for b in range(2):
                for h in range(2):
                    r = peer * TOK + h * HALF
                    value = self.dq_acc[b, r : r + HALF, :]
                    out_ref[peer, b * HALF : (b + 1) * HALF, h * HEAD : (h + 1) * HEAD] = value


def own_kernel(kown_ref, kpeer_ref, qown_ref, dk_out, dv_out, dq_out, dq_acc):
    grads = Grads((kown_ref, kpeer_ref), qown_ref, False, dk_out, dv_out, dq_acc)
    dk_out[...] = jnp.zeros_like(dk_out)
    dv_out[...] = jnp.zeros_like(dv_out)
    dq_acc[...] = jnp.zeros_like(dq_acc)
    for qhalf, khalf in ((0, 0), (1, 0), (1, 1)):
        grads.pair(qhalf, khalf)
    grads.write_queries(dq_out)


def other_kernel(
    kown_ref, kpeer_ref, qother_ref, dk_ref, dv_ref, mine_out, theirs_out, dq_out, dk_acc, dv_acc, dq_acc
):
    grads = Grads((kown_ref, kpeer_ref), qother_ref, True, dk_acc, dv_acc, dq_acc)
    dk_acc[...] = dk_ref[...]
    dv_acc[...] = dv_ref[...]
    dq_acc[...] = jnp.zeros_like(dq_acc)
    column = lax.axis_index("yl")
    for qhalf, khalf in ((1, 0), (column, column)):
        grads.pair(qhalf, khalf)
    grads.write_keys(0, mine_out)
    grads.write_keys(1, theirs_out)
    grads.write_queries(dq_out)


def merge_kernel(own_ref, got_ref, out_ref):
    out_ref[...] = (own_ref[...] + got_ref[...]).astype(BF16)


def dq_add_kernel(keep_ref, got_ref, keep_out, send_out):
    upper = lax.axis_index("x") // 2
    for j in range(2):
        mine = upper * 2 + j
        theirs = (1 - upper) * 2 + j
        keep_out[j] = keep_ref[mine] + got_ref[mine]
        send_out[j] = keep_ref[theirs] + got_ref[theirs]


def dq_half_kernel(keep_ref, got_ref, keep_out, send_out):
    odd = lax.axis_index("x") % 2
    keep_out[...] = keep_ref[odd] + got_ref[odd]
    send_out[...] = keep_ref[1 - odd] + got_ref[1 - odd]


def dq_sum_kernel(keep_ref, got_ref, out_ref):
    out_ref[...] = (keep_ref[...] + got_ref[...]).astype(BF16)


def dkv_sum_kernel(in_ref, out_ref):
    total = in_ref[0].astype(F32)
    for peer in range(1, Z):
        total += in_ref[peer].astype(F32)
    rows = total.astype(BF16)
    for peer in range(YH * X):
        out_ref[peer] = rows


def unpack_kernel(in_ref, dk_ref, dv_ref):
    for g in range(YH):
        for x in range(X):
            for b in range(2):
                at = b * HALF + x * SHARE
                dk_ref[g, at : at + SHARE, :] = in_ref[g * X + x, b * SHARE : (b + 1) * SHARE, :]
                dv_ref[g, at : at + SHARE, :] = in_ref[g * X + x, (2 + b) * SHARE : (3 + b) * SHARE, :]


def call(kernel, outs, n_in, scratch=(), flops=0, moved=1 << 20, vmem=8):
    shapes = tuple(jax.ShapeDtypeStruct(s, d) for s, d in outs)
    single = len(shapes) == 1
    return pl.pallas_call(
        kernel,
        out_shape=shapes[0] if single else shapes,
        in_specs=[VMEM_SPEC] * n_in,
        out_specs=VMEM_SPEC if single else (VMEM_SPEC,) * len(shapes),
        scratch_shapes=list(scratch),
        compiler_params=pltpu.CompilerParams(vmem_limit_bytes=vmem << 20),
        cost_estimate=pl.CostEstimate(flops=flops, bytes_accessed=moved, transcendentals=0),
    )


def exchange(value, axes):
    return lax.all_to_all(value, axes, 0, 0, tiled=True)


def shifted(value, axis, size, shift):
    return lax.ppermute(value, axis, [(i, (i + shift) % size) for i in range(size)])


def local(queries, key_codes, key_scale, value_codes, value_scale, evict_flags, out_forward, grad_output, log_norm):
    kmsg, qmsg = call(prep_kernel, [((Z, KMSG, HEAD), BF16), ((QMSG, HEAD), BF16)], 9, vmem=56)(
        key_codes,
        key_scale,
        value_codes,
        value_scale,
        evict_flags,
        queries,
        grad_output,
        out_forward,
        log_norm,
    )
    kown = exchange(kmsg, "z")
    qmine = lax.all_gather(qmsg, "x", axis=0)
    qother = shifted(qmine, "yl", YL, 1)
    kpeer = shifted(kown, "core", CORE, 1)
    work = 5 * 2 * TILE * QHALF * HEAD
    acc = ((CORE, 2, TILE, HEAD), F32)
    dq_acc = pltpu.VMEM((2, QSLOT, HEAD), F32)
    dkv_shape = ((Z, KROWS, HEAD), F32)
    piece = ((X, TOK, 2 * HEAD), F32)
    dk, dv, keep = call(own_kernel, [acc, acc, piece], 3, scratch=[dq_acc], flops=3 * work, vmem=24)(kown, kpeer, qmine)
    mine, theirs, send = call(
        other_kernel,
        [dkv_shape, dkv_shape, piece],
        5,
        scratch=[pltpu.VMEM(*acc), pltpu.VMEM(*acc), dq_acc],
        flops=2 * work,
        vmem=24,
    )(kown, kpeer, qother, dk, dv)
    dkv_got = shifted(theirs, "core", CORE, 1)
    got = shifted(send, "yl", YL, 1)
    dkv = call(merge_kernel, [((Z, KROWS, HEAD), BF16)], 2)(mine, dkv_got)
    dkv = exchange(dkv, "z")
    two = ((2, TOK, 2 * HEAD), F32)
    one = ((TOK, 2 * HEAD), F32)
    keep, send = call(dq_add_kernel, [two, two], 2)(keep, got)
    got = lax.ppermute(send, "x", [(i, i ^ 2) for i in range(X)])
    keep, send = call(dq_half_kernel, [one, one], 2)(keep, got)
    got = lax.ppermute(send, "x", [(i, i ^ 1) for i in range(X)])
    grad_queries = call(dq_sum_kernel, [((TOK, 2 * HEAD), BF16)], 2)(keep, got)
    final = call(dkv_sum_kernel, [((YH * X, KROWS, HEAD), BF16)], 1)(dkv)
    every = exchange(final, ("yh", "x"))
    grad_keys, grad_values = call(unpack_kernel, [((2, TOK, HEAD), BF16)] * 2, 1)(every)
    return grad_queries, grad_keys, grad_values


def solution(mesh):
    fine = Mesh(mesh.devices.reshape(YL, Z, CORE, YH, X), ("yl", "z", "core", "yh", "x"))
    ctx, head = ("yl", "z", "core"), ("yh", "x")
    in_specs = (
        P(ctx, head),
        P(None, ctx, None),
        P(None, ctx),
        P(None, ctx, None),
        P(None, ctx),
        P(None, ctx),
        P(ctx, head),
        P(ctx, head),
        P(head, ctx),
    )
    out_specs = (P(ctx, head), P(None, ctx, None), P(None, ctx, None))
    return jax.shard_map(local, mesh=fine, in_specs=in_specs, out_specs=out_specs, check_vma=False)
```

```python
import math

import jax
import jax.numpy as jnp
from jax import lax
from jax.experimental import pallas as pl
from jax.experimental.pallas import tpu as pltpu
from jax.sharding import Mesh
from jax.sharding import PartitionSpec as P


DELAY = 256
HEAD = 128
TOK = 128
HALF = TOK // 2
YL, Z, CORE, YH, X = 2, 16, 2, 2, 4
CHIPS = YL * Z
SHARE = HALF // X
PEERS = CORE * X
BLOCKS = 2 * CHIPS * CORE
QROWS = 512
STAT = QROWS
QMSG = QROWS + 16
KROWS = 4 * SHARE
KMSG = KROWS + 8
TILE_SRC = CHIPS // 2
TILE = TILE_SRC * SHARE
QHALF = PEERS * TOK
QSLOT = X * TOK
SCALE = HEAD**-0.5
LOG2E = math.log2(math.e)
F32 = jnp.float32
BF16 = jnp.bfloat16
VMEM_SPEC = pl.BlockSpec(memory_space=pltpu.VMEM)


def split3(value):
    first = value.astype(BF16)
    rest = value - first.astype(F32)
    second = rest.astype(BF16)
    third = (rest - second.astype(F32)).astype(BF16)
    return [first, second, third]


def prep_keys(kc_ref, ks_ref, vc_ref, vs_ref, ev_ref, kmsg_ref):
    group = lax.axis_index("yh")
    part = lax.axis_index("x")

    def dequantized(code_ref, scale_ref, start):
        codes = code_ref[group, pl.ds(start, SHARE), :].astype(F32)
        scales = scale_ref[pl.ds(group, 1), :]
        lane = lax.broadcasted_iota(jnp.int32, (SHARE, TOK), 1)
        row = lax.broadcasted_iota(jnp.int32, (SHARE, TOK), 0) + start
        column = jnp.sum(jnp.where(lane == row, scales, 0.0), axis=1, keepdims=True)
        return (codes * column).astype(BF16)

    low = pl.multiple_of(part * SHARE, SHARE)
    high = pl.multiple_of(HALF + part * SHARE, SHARE)
    flags = jnp.broadcast_to(ev_ref[pl.ds(group, 1), :], (8, TOK)).astype(F32).astype(BF16)
    rows = jnp.concatenate(
        [
            dequantized(kc_ref, ks_ref, low),
            dequantized(kc_ref, ks_ref, high),
            dequantized(vc_ref, vs_ref, low),
            dequantized(vc_ref, vs_ref, high),
        ],
        axis=0,
    )
    for peer in range(Z):
        kmsg_ref[peer, 0:KROWS, :] = rows
        kmsg_ref[peer, KROWS:KMSG, :] = flags


def prep_queries(q_ref, do_ref, out_ref, norm_ref, qmsg_ref):
    q = q_ref[...]
    do = do_ref[...]
    product = do.astype(F32) * out_ref[...].astype(F32)
    norm = norm_ref[...] * LOG2E
    delta = jnp.concatenate(
        [jnp.sum(product[:, h * HEAD : (h + 1) * HEAD].T, axis=0, keepdims=True) for h in range(2)], axis=0
    )

    def halves(stat):
        return [
            jnp.concatenate([stat[0:1, b * HALF : (b + 1) * HALF], stat[1:2, b * HALF : (b + 1) * HALF]], axis=1)
            for b in range(2)
        ]

    norm_half, delta_half = halves(norm), halves(delta)
    stats = []
    for b in range(2):
        stats += split3(norm_half[b]) + split3(delta_half[b])
    stats = [s.astype(F32) for s in stats] + [jnp.zeros((4, TOK), F32)]
    stats = jnp.concatenate(stats, axis=0).astype(BF16)

    def reordered(value):
        return jnp.concatenate(
            [value[b * HALF : (b + 1) * HALF, h * HEAD : (h + 1) * HEAD] for b in range(2) for h in range(2)],
            axis=0,
        )

    qmsg_ref[0:256, :] = reordered(q)
    qmsg_ref[256:512, :] = reordered(do)
    qmsg_ref[QROWS:QMSG, :] = stats


def prep_kernel(
    kc_ref, ks_ref, vc_ref, vs_ref, ev_ref, q_ref, do_ref, out_ref, norm_ref, kmsg_ref, qmsg_ref
):
    prep_keys(kc_ref, ks_ref, vc_ref, vs_ref, ev_ref, kmsg_ref)
    prep_queries(q_ref, do_ref, out_ref, norm_ref, qmsg_ref)


class Grads:
    def __init__(self, kmsg_refs, qmsg_ref, other, dk_acc, dv_acc, dq_acc):
        self.kmsg_refs, self.qmsg_ref = kmsg_refs, qmsg_ref
        self.dk_acc, self.dv_acc, self.dq_acc = dk_acc, dv_acc, dq_acc
        self.core = lax.axis_index("core")
        self.part = lax.axis_index("x")
        self.column = lax.axis_index("yl")
        self.chip = (1 - self.column if other else self.column) * Z + lax.axis_index("z")

    def keys(self, slot, khalf):
        kmsg_ref = self.kmsg_refs[slot]
        core = self.core if slot == 0 else 1 - self.core
        index = lax.broadcasted_iota(jnp.int32, (TILE, 1), 0)
        src = self.column * Z + index // SHARE
        block = jnp.where(khalf == 0, CORE * src + core, BLOCKS - 1 - CORE * src - core)
        offset = self.part * SHARE + index % SHARE
        pos = block * HALF + offset
        flags = kmsg_ref[:, KROWS : KROWS + 8, :][:, 0, :].astype(F32)
        wide = jnp.broadcast_to(flags[:, None, :], (Z, SHARE, TOK)).reshape(TILE, TOK)
        lane = lax.broadcasted_iota(jnp.int32, (TILE, TOK), 1)
        flag = jnp.sum(jnp.where(lane == khalf * HALF + offset, wide, 0.0), axis=1, keepdims=True)
        last = jnp.where(flag > 0.5, pos + DELAY - 1, BLOCKS * HALF)
        krow = pl.multiple_of(khalf * SHARE, SHARE)
        vrow = pl.multiple_of((2 + khalf) * SHARE, SHARE)
        k = kmsg_ref[:, pl.ds(krow, SHARE), :].reshape(TILE, HEAD)
        v = kmsg_ref[:, pl.ds(vrow, SHARE), :].reshape(TILE, HEAD)
        return k, v, pos, last

    def stat_row(self, qmsg_ref, qhalf, which):
        rows = []
        for peer in range(X):
            both = qmsg_ref[peer, STAT : STAT + 16, :].astype(F32)

            def total(b):
                at = b * 6 + which * 3
                return both[at : at + 1] + both[at + 1 : at + 2] + both[at + 2 : at + 3]

            rows.append(jnp.where(qhalf == 0, total(0), total(1)))
        return jnp.concatenate(rows, axis=1)

    def pair(self, qhalf, khalf, slots=(0, 1)):
        q0 = pl.multiple_of(qhalf * TOK, TOK)
        d0 = pl.multiple_of((2 + qhalf) * TOK, TOK)
        norm = self.stat_row(self.qmsg_ref, qhalf, 0)
        delta = self.stat_row(self.qmsg_ref, qhalf, 1)
        qblock = jnp.where(qhalf == 0, CORE * self.chip + self.core, BLOCKS - 1 - CORE * self.chip - self.core)
        qpos = qblock * HALF + lax.broadcasted_iota(jnp.int32, (1, QSLOT), 1) % HALF
        q = self.qmsg_ref[:, pl.ds(q0, TOK), :].reshape(QSLOT, HEAD)
        do = self.qmsg_ref[:, pl.ds(d0, TOK), :].reshape(QSLOT, HEAD)
        for slot in slots:
            k, v, kpos, klast = self.keys(slot, khalf)
            s = lax.dot_general(k, q, (((1,), (1,)), ((), ())), preferred_element_type=F32)
            dp = lax.dot_general(v, do, (((1,), (1,)), ((), ())), preferred_element_type=F32)
            seen = (kpos <= qpos) & (qpos <= klast)
            w = jnp.where(seen, jnp.exp2(s * (SCALE * LOG2E) - norm), 0.0)
            ds = ((w * SCALE) * (dp - delta)).astype(BF16)
            wb = w.astype(BF16)
            self.dv_acc[slot, khalf] += jnp.dot(wb, do, preferred_element_type=F32)
            self.dk_acc[slot, khalf] += jnp.dot(ds, q, preferred_element_type=F32)
            self.dq_acc[qhalf] += lax.dot_general(ds, k, (((0,), (0,)), ((), ())), preferred_element_type=F32)

    def write_keys(self, slot, out_ref):
        for khalf in range(2):
            dk = self.dk_acc[slot, khalf].reshape(Z, SHARE, HEAD)
            dv = self.dv_acc[slot, khalf].reshape(Z, SHARE, HEAD)
            out_ref[:, khalf * SHARE : (khalf + 1) * SHARE, :] = dk
            out_ref[:, (2 + khalf) * SHARE : (3 + khalf) * SHARE, :] = dv

    def write_queries(self, out_ref):
        for peer in range(X):
            for b in range(2):
                for h in range(2):
                    r = peer * TOK + h * HALF
                    value = self.dq_acc[b, r : r + HALF, :]
                    out_ref[peer, b * HALF : (b + 1) * HALF, h * HEAD : (h + 1) * HEAD] = value


OWN_PAIRS = ((0, 0), (1, 0), (1, 1))


def own_first_kernel(kown_ref, qown_ref, dk_out, dv_out, dq_out):
    grads = Grads((kown_ref,), qown_ref, False, dk_out, dv_out, dq_out)
    dk_out[...] = jnp.zeros_like(dk_out)
    dv_out[...] = jnp.zeros_like(dv_out)
    dq_out[...] = jnp.zeros_like(dq_out)
    for qhalf, khalf in OWN_PAIRS:
        grads.pair(qhalf, khalf, (0,))


def own_second_kernel(kpeer_ref, qown_ref, dq_ref, dk_out, dv_out, dq_out, dq_acc):
    grads = Grads((None, kpeer_ref), qown_ref, False, {}, {}, dq_acc)
    dk_out[...] = jnp.zeros_like(dk_out)
    dv_out[...] = jnp.zeros_like(dv_out)
    dq_acc[...] = dq_ref[...]
    grads.dk_acc, grads.dv_acc = Shifted(dk_out), Shifted(dv_out)
    for qhalf, khalf in OWN_PAIRS:
        grads.pair(qhalf, khalf, (1,))
    grads.write_queries(dq_out)


class Shifted:
    def __init__(self, ref):
        self.ref = ref

    def __getitem__(self, index):
        return self.ref[index[0] - 1, index[1]]

    def __setitem__(self, index, value):
        self.ref[index[0] - 1, index[1]] = value


def other_kernel(
    kown_ref,
    kpeer_ref,
    qother_ref,
    dk0_ref,
    dv0_ref,
    dk1_ref,
    dv1_ref,
    mine_out,
    theirs_out,
    dq_out,
    dk_acc,
    dv_acc,
    dq_acc,
):
    grads = Grads((kown_ref, kpeer_ref), qother_ref, True, dk_acc, dv_acc, dq_acc)
    dk_acc[0] = dk0_ref[0]
    dk_acc[1] = dk1_ref[0]
    dv_acc[0] = dv0_ref[0]
    dv_acc[1] = dv1_ref[0]
    dq_acc[...] = jnp.zeros_like(dq_acc)
    column = lax.axis_index("yl")
    for qhalf, khalf in ((1, 0), (column, column)):
        grads.pair(qhalf, khalf)
    grads.write_keys(0, mine_out)
    grads.write_keys(1, theirs_out)
    grads.write_queries(dq_out)


def merge_kernel(own_ref, got_ref, out_ref):
    out_ref[...] = (own_ref[...] + got_ref[...]).astype(BF16)


def dq_add_kernel(keep_ref, got_ref, keep_out, send_out):
    upper = lax.axis_index("x") // 2
    for j in range(2):
        mine = upper * 2 + j
        theirs = (1 - upper) * 2 + j
        keep_out[j] = keep_ref[mine] + got_ref[mine]
        send_out[j] = keep_ref[theirs] + got_ref[theirs]


def dq_half_kernel(keep_ref, got_ref, keep_out, send_out):
    odd = lax.axis_index("x") % 2
    keep_out[...] = keep_ref[odd] + got_ref[odd]
    send_out[...] = keep_ref[1 - odd] + got_ref[1 - odd]


def dq_sum_kernel(keep_ref, got_ref, out_ref):
    out_ref[...] = (keep_ref[...] + got_ref[...]).astype(BF16)


def dkv_sum_kernel(in_ref, out_ref):
    total = in_ref[0].astype(F32)
    for peer in range(1, Z):
        total += in_ref[peer].astype(F32)
    rows = total.astype(BF16)
    for peer in range(YH * X):
        out_ref[peer] = rows


def unpack_kernel(in_ref, dk_ref, dv_ref):
    for g in range(YH):
        for x in range(X):
            for b in range(2):
                at = b * HALF + x * SHARE
                dk_ref[g, at : at + SHARE, :] = in_ref[g * X + x, b * SHARE : (b + 1) * SHARE, :]
                dv_ref[g, at : at + SHARE, :] = in_ref[g * X + x, (2 + b) * SHARE : (3 + b) * SHARE, :]


def call(kernel, outs, n_in, scratch=(), flops=0, moved=1 << 20, vmem=8):
    shapes = tuple(jax.ShapeDtypeStruct(s, d) for s, d in outs)
    single = len(shapes) == 1
    return pl.pallas_call(
        kernel,
        out_shape=shapes[0] if single else shapes,
        in_specs=[VMEM_SPEC] * n_in,
        out_specs=VMEM_SPEC if single else (VMEM_SPEC,) * len(shapes),
        scratch_shapes=list(scratch),
        compiler_params=pltpu.CompilerParams(vmem_limit_bytes=vmem << 20),
        cost_estimate=pl.CostEstimate(flops=flops, bytes_accessed=moved, transcendentals=0),
    )


def exchange(value, axes):
    return lax.all_to_all(value, axes, 0, 0, tiled=True)


def shifted(value, axis, size, shift):
    return lax.ppermute(value, axis, [(i, (i + shift) % size) for i in range(size)])


def local(queries, key_codes, key_scale, value_codes, value_scale, evict_flags, out_forward, grad_output, log_norm):
    kmsg, qmsg = call(prep_kernel, [((Z, KMSG, HEAD), BF16), ((QMSG, HEAD), BF16)], 9, vmem=56)(
        key_codes,
        key_scale,
        value_codes,
        value_scale,
        evict_flags,
        queries,
        grad_output,
        out_forward,
        log_norm,
    )
    kown = exchange(kmsg, "z")
    qmine = lax.all_gather(qmsg, "x", axis=0)
    qother = shifted(qmine, "yl", YL, 1)
    kpeer = shifted(kown, "core", CORE, 1)
    work = 5 * 2 * TILE * QHALF * HEAD
    acc = ((CORE, 2, TILE, HEAD), F32)
    half_acc = ((1, 2, TILE, HEAD), F32)
    dq_acc = ((2, QSLOT, HEAD), F32)
    dkv_shape = ((Z, KROWS, HEAD), F32)
    piece = ((X, TOK, 2 * HEAD), F32)
    dk0, dv0, dq = call(own_first_kernel, [half_acc, half_acc, dq_acc], 2, flops=work * 3 // 2, vmem=24)(kown, qmine)
    dk1, dv1, keep = call(
        own_second_kernel, [half_acc, half_acc, piece], 3, scratch=[pltpu.VMEM(*dq_acc)], flops=work * 3 // 2, vmem=24
    )(kpeer, qmine, dq)
    mine, theirs, send = call(
        other_kernel,
        [dkv_shape, dkv_shape, piece],
        7,
        scratch=[pltpu.VMEM(*acc), pltpu.VMEM(*acc), pltpu.VMEM(*dq_acc)],
        flops=2 * work,
        vmem=24,
    )(kown, kpeer, qother, dk0, dv0, dk1, dv1)
    dkv_got = shifted(theirs, "core", CORE, 1)
    got = shifted(send, "yl", YL, 1)
    dkv = call(merge_kernel, [((Z, KROWS, HEAD), BF16)], 2)(mine, dkv_got)
    dkv = exchange(dkv, "z")
    two = ((2, TOK, 2 * HEAD), F32)
    one = ((TOK, 2 * HEAD), F32)
    keep, send = call(dq_add_kernel, [two, two], 2)(keep, got)
    got = lax.ppermute(send, "x", [(i, i ^ 2) for i in range(X)])
    keep, send = call(dq_half_kernel, [one, one], 2)(keep, got)
    got = lax.ppermute(send, "x", [(i, i ^ 1) for i in range(X)])
    grad_queries = call(dq_sum_kernel, [((TOK, 2 * HEAD), BF16)], 2)(keep, got)
    final = call(dkv_sum_kernel, [((YH * X, KROWS, HEAD), BF16)], 1)(dkv)
    every = exchange(final, ("yh", "x"))
    grad_keys, grad_values = call(unpack_kernel, [((2, TOK, HEAD), BF16)] * 2, 1)(every)
    return grad_queries, grad_keys, grad_values


def solution(mesh):
    fine = Mesh(mesh.devices.reshape(YL, Z, CORE, YH, X), ("yl", "z", "core", "yh", "x"))
    ctx, head = ("yl", "z", "core"), ("yh", "x")
    in_specs = (
        P(ctx, head),
        P(None, ctx, None),
        P(None, ctx),
        P(None, ctx, None),
        P(None, ctx),
        P(None, ctx),
        P(ctx, head),
        P(ctx, head),
        P(head, ctx),
    )
    out_specs = (P(ctx, head), P(None, ctx, None), P(None, ctx, None))
    return jax.shard_map(local, mesh=fine, in_specs=in_specs, out_specs=out_specs, check_vma=False)
```

```python
import math

import jax
import jax.numpy as jnp
from jax import lax
from jax.experimental import pallas as pl
from jax.experimental.pallas import tpu as pltpu
from jax.sharding import Mesh
from jax.sharding import PartitionSpec as P


DELAY = 256
HEAD = 128
TOK = 128
HALF = TOK // 2
YL, Z, CORE, YH, X = 2, 16, 2, 2, 4
CHIPS = YL * Z
SHARE = HALF // X
PEERS = CORE * X
BLOCKS = 2 * CHIPS * CORE
QROWS = 512
STAT = QROWS
QMSG = QROWS + 16
KROWS = 4 * SHARE
KMSG = KROWS + 8
TILE_SRC = CHIPS // 2
TILE = TILE_SRC * SHARE
QHALF = PEERS * TOK
QSLOT = X * TOK
SCALE = HEAD**-0.5
LOG2E = math.log2(math.e)
F32 = jnp.float32
BF16 = jnp.bfloat16
VMEM_SPEC = pl.BlockSpec(memory_space=pltpu.VMEM)


def split3(value):
    first = value.astype(BF16)
    rest = value - first.astype(F32)
    second = rest.astype(BF16)
    third = (rest - second.astype(F32)).astype(BF16)
    return [first, second, third]


def prep_keys(kc_ref, ks_ref, vc_ref, vs_ref, ev_ref, kmsg_ref):
    group = lax.axis_index("yh")
    part = lax.axis_index("x")

    def dequantized(code_ref, scale_ref, start):
        codes = code_ref[group, pl.ds(start, SHARE), :].astype(F32)
        scales = scale_ref[pl.ds(group, 1), :]
        lane = lax.broadcasted_iota(jnp.int32, (SHARE, TOK), 1)
        row = lax.broadcasted_iota(jnp.int32, (SHARE, TOK), 0) + start
        column = jnp.sum(jnp.where(lane == row, scales, 0.0), axis=1, keepdims=True)
        return (codes * column).astype(BF16)

    low = pl.multiple_of(part * SHARE, SHARE)
    high = pl.multiple_of(HALF + part * SHARE, SHARE)
    flags = jnp.broadcast_to(ev_ref[pl.ds(group, 1), :], (8, TOK)).astype(F32).astype(BF16)
    rows = jnp.concatenate(
        [
            dequantized(kc_ref, ks_ref, low),
            dequantized(kc_ref, ks_ref, high),
            dequantized(vc_ref, vs_ref, low),
            dequantized(vc_ref, vs_ref, high),
        ],
        axis=0,
    )
    for peer in range(Z):
        kmsg_ref[peer, 0:KROWS, :] = rows
        kmsg_ref[peer, KROWS:KMSG, :] = flags


def prep_queries(q_ref, do_ref, out_ref, norm_ref, qmsg_ref):
    q = q_ref[...]
    do = do_ref[...]
    product = do.astype(F32) * out_ref[...].astype(F32)
    norm = norm_ref[...] * LOG2E
    delta = jnp.concatenate(
        [jnp.sum(product[:, h * HEAD : (h + 1) * HEAD].T, axis=0, keepdims=True) for h in range(2)], axis=0
    )

    def halves(stat):
        return [
            jnp.concatenate([stat[0:1, b * HALF : (b + 1) * HALF], stat[1:2, b * HALF : (b + 1) * HALF]], axis=1)
            for b in range(2)
        ]

    norm_half, delta_half = halves(norm), halves(delta)
    stats = []
    for b in range(2):
        stats += split3(norm_half[b]) + split3(delta_half[b])
    stats = [s.astype(F32) for s in stats] + [jnp.zeros((4, TOK), F32)]
    stats = jnp.concatenate(stats, axis=0).astype(BF16)

    def reordered(value):
        return jnp.concatenate(
            [value[b * HALF : (b + 1) * HALF, h * HEAD : (h + 1) * HEAD] for b in range(2) for h in range(2)],
            axis=0,
        )

    qmsg_ref[0:256, :] = reordered(q)
    qmsg_ref[256:512, :] = reordered(do)
    qmsg_ref[QROWS:QMSG, :] = stats


def prep_kernel(
    kc_ref, ks_ref, vc_ref, vs_ref, ev_ref, q_ref, do_ref, out_ref, norm_ref, kmsg_ref, qmsg_ref
):
    prep_keys(kc_ref, ks_ref, vc_ref, vs_ref, ev_ref, kmsg_ref)
    prep_queries(q_ref, do_ref, out_ref, norm_ref, qmsg_ref)


class Grads:
    def __init__(self, kmsg_refs, qmsg_ref, other, dk_acc, dv_acc, dq_acc):
        self.kmsg_refs, self.qmsg_ref = kmsg_refs, qmsg_ref
        self.dk_acc, self.dv_acc, self.dq_acc = dk_acc, dv_acc, dq_acc
        self.core = lax.axis_index("core")
        self.part = lax.axis_index("x")
        self.column = lax.axis_index("yl")
        self.chip = (1 - self.column if other else self.column) * Z + lax.axis_index("z")

    def keys(self, slot, khalf):
        kmsg_ref = self.kmsg_refs[slot]
        core = self.core if slot == 0 else 1 - self.core
        index = lax.broadcasted_iota(jnp.int32, (TILE, 1), 0)
        src = self.column * Z + index // SHARE
        block = jnp.where(khalf == 0, CORE * src + core, BLOCKS - 1 - CORE * src - core)
        offset = self.part * SHARE + index % SHARE
        pos = block * HALF + offset
        flags = kmsg_ref[:, KROWS : KROWS + 8, :][:, 0, :].astype(F32)
        wide = jnp.broadcast_to(flags[:, None, :], (Z, SHARE, TOK)).reshape(TILE, TOK)
        lane = lax.broadcasted_iota(jnp.int32, (TILE, TOK), 1)
        flag = jnp.sum(jnp.where(lane == khalf * HALF + offset, wide, 0.0), axis=1, keepdims=True)
        last = jnp.where(flag > 0.5, pos + DELAY - 1, BLOCKS * HALF)
        krow = pl.multiple_of(khalf * SHARE, SHARE)
        vrow = pl.multiple_of((2 + khalf) * SHARE, SHARE)
        k = kmsg_ref[:, pl.ds(krow, SHARE), :].reshape(TILE, HEAD)
        v = kmsg_ref[:, pl.ds(vrow, SHARE), :].reshape(TILE, HEAD)
        return k, v, pos, last

    def stat_row(self, qmsg_ref, qhalf, which):
        rows = []
        for peer in range(X):
            both = qmsg_ref[peer, STAT : STAT + 16, :].astype(F32)

            def total(b):
                at = b * 6 + which * 3
                return both[at : at + 1] + both[at + 1 : at + 2] + both[at + 2 : at + 3]

            rows.append(jnp.where(qhalf == 0, total(0), total(1)))
        return jnp.concatenate(rows, axis=1)

    def pair(self, qhalf, khalf, slots=(0, 1)):
        q0 = pl.multiple_of(qhalf * TOK, TOK)
        d0 = pl.multiple_of((2 + qhalf) * TOK, TOK)
        norm = self.stat_row(self.qmsg_ref, qhalf, 0)
        delta = self.stat_row(self.qmsg_ref, qhalf, 1)
        qblock = jnp.where(qhalf == 0, CORE * self.chip + self.core, BLOCKS - 1 - CORE * self.chip - self.core)
        qpos = qblock * HALF + lax.broadcasted_iota(jnp.int32, (1, QSLOT), 1) % HALF
        q = self.qmsg_ref[:, pl.ds(q0, TOK), :].reshape(QSLOT, HEAD)
        do = self.qmsg_ref[:, pl.ds(d0, TOK), :].reshape(QSLOT, HEAD)
        for slot in slots:
            k, v, kpos, klast = self.keys(slot, khalf)
            s = lax.dot_general(k, q, (((1,), (1,)), ((), ())), preferred_element_type=F32)
            dp = lax.dot_general(v, do, (((1,), (1,)), ((), ())), preferred_element_type=F32)
            seen = (kpos <= qpos) & (qpos <= klast)
            w = jnp.where(seen, jnp.exp2(s * (SCALE * LOG2E) - norm), 0.0)
            ds = ((w * SCALE) * (dp - delta)).astype(BF16)
            wb = w.astype(BF16)
            self.dv_acc[slot, khalf] += jnp.dot(wb, do, preferred_element_type=F32)
            self.dk_acc[slot, khalf] += jnp.dot(ds, q, preferred_element_type=F32)
            self.dq_acc[qhalf] += lax.dot_general(ds, k, (((0,), (0,)), ((), ())), preferred_element_type=F32)

    def write_keys(self, slot, out_ref):
        for khalf in range(2):
            dk = self.dk_acc[slot, khalf].reshape(Z, SHARE, HEAD)
            dv = self.dv_acc[slot, khalf].reshape(Z, SHARE, HEAD)
            out_ref[:, khalf * SHARE : (khalf + 1) * SHARE, :] = dk
            out_ref[:, (2 + khalf) * SHARE : (3 + khalf) * SHARE, :] = dv

    def write_queries(self, out_ref):
        for peer in range(X):
            for b in range(2):
                for h in range(2):
                    r = peer * TOK + h * HALF
                    value = self.dq_acc[b, r : r + HALF, :]
                    out_ref[peer, b * HALF : (b + 1) * HALF, h * HEAD : (h + 1) * HEAD] = value


OWN_PAIRS = ((0, 0), (1, 0), (1, 1))


def own_first_kernel(kown_ref, qown_ref, dk_out, dv_out, dq_out):
    grads = Grads((kown_ref,), qown_ref, False, dk_out, dv_out, dq_out)
    dk_out[...] = jnp.zeros_like(dk_out)
    dv_out[...] = jnp.zeros_like(dv_out)
    dq_out[...] = jnp.zeros_like(dq_out)
    for qhalf, khalf in OWN_PAIRS:
        grads.pair(qhalf, khalf, (0,))


def own_second_kernel(kpeer_ref, qown_ref, dq_ref, dk_out, dv_out, dq_out, dq_acc):
    grads = Grads((None, kpeer_ref), qown_ref, False, {}, {}, dq_acc)
    dk_out[...] = jnp.zeros_like(dk_out)
    dv_out[...] = jnp.zeros_like(dv_out)
    dq_acc[...] = dq_ref[...]
    grads.dk_acc, grads.dv_acc = Shifted(dk_out), Shifted(dv_out)
    for qhalf, khalf in OWN_PAIRS:
        grads.pair(qhalf, khalf, (1,))
    grads.write_queries(dq_out)


class Shifted:
    def __init__(self, ref):
        self.ref = ref

    def __getitem__(self, index):
        return self.ref[index[0] - 1, index[1]]

    def __setitem__(self, index, value):
        self.ref[index[0] - 1, index[1]] = value


def other_kernel(
    kown_ref,
    kpeer_ref,
    qother_ref,
    dk0_ref,
    dv0_ref,
    dk1_ref,
    dv1_ref,
    mine_out,
    theirs_out,
    dq_out,
    dk_acc,
    dv_acc,
    dq_acc,
):
    grads = Grads((kown_ref, kpeer_ref), qother_ref, True, dk_acc, dv_acc, dq_acc)
    dk_acc[0] = dk0_ref[0]
    dk_acc[1] = dk1_ref[0]
    dv_acc[0] = dv0_ref[0]
    dv_acc[1] = dv1_ref[0]
    dq_acc[...] = jnp.zeros_like(dq_acc)
    column = lax.axis_index("yl")
    for qhalf, khalf in ((1, 0), (column, column)):
        grads.pair(qhalf, khalf)
    grads.write_keys(0, mine_out)
    grads.write_keys(1, theirs_out)
    grads.write_queries(dq_out)


def merge_kernel(own_ref, got_ref, out_ref):
    out_ref[...] = (own_ref[...] + got_ref[...]).astype(BF16)


def dq_add_kernel(keep_ref, got_ref, *out_refs):
    part = lax.axis_index("x")
    for shift in range(X):
        to = (part + shift) % X
        out_refs[shift][...] = keep_ref[to] + got_ref[to]


def dq_sum_kernel(*refs):
    *in_refs, out_ref = refs
    total = in_refs[0][...]
    for ref in in_refs[1:]:
        total += ref[...]
    out_ref[...] = total.astype(BF16)


def dkv_sum_kernel(in_ref, out_ref):
    total = in_ref[0].astype(F32)
    for peer in range(1, Z):
        total += in_ref[peer].astype(F32)
    rows = total.astype(BF16)
    for peer in range(YH * X):
        out_ref[peer] = rows


def unpack_kernel(in_ref, dk_ref, dv_ref):
    for g in range(YH):
        for x in range(X):
            for b in range(2):
                at = b * HALF + x * SHARE
                dk_ref[g, at : at + SHARE, :] = in_ref[g * X + x, b * SHARE : (b + 1) * SHARE, :]
                dv_ref[g, at : at + SHARE, :] = in_ref[g * X + x, (2 + b) * SHARE : (3 + b) * SHARE, :]


def call(kernel, outs, n_in, scratch=(), flops=0, moved=1 << 20, vmem=8):
    shapes = tuple(jax.ShapeDtypeStruct(s, d) for s, d in outs)
    single = len(shapes) == 1
    return pl.pallas_call(
        kernel,
        out_shape=shapes[0] if single else shapes,
        in_specs=[VMEM_SPEC] * n_in,
        out_specs=VMEM_SPEC if single else (VMEM_SPEC,) * len(shapes),
        scratch_shapes=list(scratch),
        compiler_params=pltpu.CompilerParams(vmem_limit_bytes=vmem << 20),
        cost_estimate=pl.CostEstimate(flops=flops, bytes_accessed=moved, transcendentals=0),
    )


def exchange(value, axes):
    return lax.all_to_all(value, axes, 0, 0, tiled=True)


def shifted(value, axis, size, shift):
    return lax.ppermute(value, axis, [(i, (i + shift) % size) for i in range(size)])


def local(queries, key_codes, key_scale, value_codes, value_scale, evict_flags, out_forward, grad_output, log_norm):
    kmsg, qmsg = call(prep_kernel, [((Z, KMSG, HEAD), BF16), ((QMSG, HEAD), BF16)], 9, vmem=56)(
        key_codes,
        key_scale,
        value_codes,
        value_scale,
        evict_flags,
        queries,
        grad_output,
        out_forward,
        log_norm,
    )
    kown = exchange(kmsg, "z")
    qmine = lax.all_gather(qmsg, "x", axis=0)
    qother = shifted(qmine, "yl", YL, 1)
    kpeer = shifted(kown, "core", CORE, 1)
    work = 5 * 2 * TILE * QHALF * HEAD
    acc = ((CORE, 2, TILE, HEAD), F32)
    half_acc = ((1, 2, TILE, HEAD), F32)
    dq_acc = ((2, QSLOT, HEAD), F32)
    dkv_shape = ((Z, KROWS, HEAD), F32)
    piece = ((X, TOK, 2 * HEAD), F32)
    dk0, dv0, dq = call(own_first_kernel, [half_acc, half_acc, dq_acc], 2, flops=work * 3 // 2, vmem=24)(kown, qmine)
    dk1, dv1, keep = call(
        own_second_kernel, [half_acc, half_acc, piece], 3, scratch=[pltpu.VMEM(*dq_acc)], flops=work * 3 // 2, vmem=24
    )(kpeer, qmine, dq)
    mine, theirs, send = call(
        other_kernel,
        [dkv_shape, dkv_shape, piece],
        7,
        scratch=[pltpu.VMEM(*acc), pltpu.VMEM(*acc), pltpu.VMEM(*dq_acc)],
        flops=2 * work,
        vmem=24,
    )(kown, kpeer, qother, dk0, dv0, dk1, dv1)
    dkv_got = shifted(theirs, "core", CORE, 1)
    got = shifted(send, "yl", YL, 1)
    dkv = call(merge_kernel, [((Z, KROWS, HEAD), BF16)], 2)(mine, dkv_got)
    dkv = exchange(dkv, "z")
    parts = call(dq_add_kernel, [((TOK, 2 * HEAD), F32)] * X, 2)(keep, got)
    home = [parts[0]]
    for k in range(1, X):
        home.append(shifted(parts[k], "x", X, k))
    grad_queries = call(dq_sum_kernel, [((TOK, 2 * HEAD), BF16)], X)(*home)
    final = call(dkv_sum_kernel, [((YH * X, KROWS, HEAD), BF16)], 1)(dkv)
    every = exchange(final, ("yh", "x"))
    grad_keys, grad_values = call(unpack_kernel, [((2, TOK, HEAD), BF16)] * 2, 1)(every)
    return grad_queries, grad_keys, grad_values


def solution(mesh):
    fine = Mesh(mesh.devices.reshape(YL, Z, CORE, YH, X), ("yl", "z", "core", "yh", "x"))
    ctx, head = ("yl", "z", "core"), ("yh", "x")
    in_specs = (
        P(ctx, head),
        P(None, ctx, None),
        P(None, ctx),
        P(None, ctx, None),
        P(None, ctx),
        P(None, ctx),
        P(ctx, head),
        P(ctx, head),
        P(head, ctx),
    )
    out_specs = (P(ctx, head), P(None, ctx, None), P(None, ctx, None))
    return jax.shard_map(local, mesh=fine, in_specs=in_specs, out_specs=out_specs, check_vma=False)
```

```python
import math

import jax
import jax.numpy as jnp
from jax import lax
from jax.experimental import pallas as pl
from jax.experimental.pallas import tpu as pltpu
from jax.sharding import Mesh
from jax.sharding import PartitionSpec as P


DELAY = 256
HEAD = 128
TOK = 128
HALF = TOK // 2
YL, Z, CORE, YH, X = 2, 16, 2, 2, 4
CHIPS = YL * Z
SHARE = HALF // X
PEERS = CORE * X
BLOCKS = 2 * CHIPS * CORE
QROWS = 512
STAT = QROWS
QMSG = QROWS + 16
KROWS = 4 * SHARE
KMSG = KROWS + 8
TILE_SRC = CHIPS // 2
TILE = TILE_SRC * SHARE
QHALF = PEERS * TOK
QSLOT = X * TOK
SCALE = HEAD**-0.5
LOG2E = math.log2(math.e)
F32 = jnp.float32
BF16 = jnp.bfloat16
VMEM_SPEC = pl.BlockSpec(memory_space=pltpu.VMEM)


def split3(value):
    first = value.astype(BF16)
    rest = value - first.astype(F32)
    second = rest.astype(BF16)
    third = (rest - second.astype(F32)).astype(BF16)
    return [first, second, third]


def prep_keys(kc_ref, ks_ref, vc_ref, vs_ref, ev_ref, kmsg_ref):
    group = lax.axis_index("yh")
    part = lax.axis_index("x")

    def dequantized(code_ref, scale_ref, start):
        codes = code_ref[group, pl.ds(start, SHARE), :].astype(F32)
        scales = scale_ref[pl.ds(group, 1), :]
        lane = lax.broadcasted_iota(jnp.int32, (SHARE, TOK), 1)
        row = lax.broadcasted_iota(jnp.int32, (SHARE, TOK), 0) + start
        column = jnp.sum(jnp.where(lane == row, scales, 0.0), axis=1, keepdims=True)
        return (codes * column).astype(BF16)

    low = pl.multiple_of(part * SHARE, SHARE)
    high = pl.multiple_of(HALF + part * SHARE, SHARE)
    flags = jnp.broadcast_to(ev_ref[pl.ds(group, 1), :], (8, TOK)).astype(F32).astype(BF16)
    rows = jnp.concatenate(
        [
            dequantized(kc_ref, ks_ref, low),
            dequantized(kc_ref, ks_ref, high),
            dequantized(vc_ref, vs_ref, low),
            dequantized(vc_ref, vs_ref, high),
        ],
        axis=0,
    )
    for peer in range(Z):
        kmsg_ref[peer, 0:KROWS, :] = rows
        kmsg_ref[peer, KROWS:KMSG, :] = flags


def prep_queries(q_ref, do_ref, out_ref, norm_ref, qmsg_ref):
    q = q_ref[...]
    do = do_ref[...]
    product = do.astype(F32) * out_ref[...].astype(F32)
    norm = norm_ref[...] * LOG2E
    delta = jnp.concatenate(
        [jnp.sum(product[:, h * HEAD : (h + 1) * HEAD].T, axis=0, keepdims=True) for h in range(2)], axis=0
    )

    def halves(stat):
        return [
            jnp.concatenate([stat[0:1, b * HALF : (b + 1) * HALF], stat[1:2, b * HALF : (b + 1) * HALF]], axis=1)
            for b in range(2)
        ]

    norm_half, delta_half = halves(norm), halves(delta)
    stats = []
    for b in range(2):
        stats += split3(norm_half[b]) + split3(delta_half[b])
    stats = [s.astype(F32) for s in stats] + [jnp.zeros((4, TOK), F32)]
    stats = jnp.concatenate(stats, axis=0).astype(BF16)

    def reordered(value):
        return jnp.concatenate(
            [value[b * HALF : (b + 1) * HALF, h * HEAD : (h + 1) * HEAD] for b in range(2) for h in range(2)],
            axis=0,
        )

    qmsg_ref[0:256, :] = reordered(q)
    qmsg_ref[256:512, :] = reordered(do)
    qmsg_ref[QROWS:QMSG, :] = stats


def prep_kernel(
    kc_ref, ks_ref, vc_ref, vs_ref, ev_ref, q_ref, do_ref, out_ref, norm_ref, kmsg_ref, qmsg_ref
):
    prep_keys(kc_ref, ks_ref, vc_ref, vs_ref, ev_ref, kmsg_ref)
    prep_queries(q_ref, do_ref, out_ref, norm_ref, qmsg_ref)


class Grads:
    def __init__(self, kmsg_refs, qmsg_ref, other, dk_acc, dv_acc, dq_acc):
        self.kmsg_refs, self.qmsg_ref, self.other = kmsg_refs, qmsg_ref, other
        self.dk_acc, self.dv_acc, self.dq_acc = dk_acc, dv_acc, dq_acc
        self.core = lax.axis_index("core")
        self.part = lax.axis_index("x")
        self.column = lax.axis_index("yl")
        self.chip = (1 - self.column if other else self.column) * Z + lax.axis_index("z")

    def keys(self, slot, khalf):
        kmsg_ref = self.kmsg_refs[slot]
        core = self.core if slot == 0 else 1 - self.core
        index = lax.broadcasted_iota(jnp.int32, (TILE, 1), 0)
        src = self.column * Z + index // SHARE
        block = jnp.where(khalf == 0, CORE * src + core, BLOCKS - 1 - CORE * src - core)
        offset = self.part * SHARE + index % SHARE
        pos = block * HALF + offset
        flags = kmsg_ref[:, KROWS : KROWS + 8, :][:, 0, :].astype(F32)
        wide = jnp.broadcast_to(flags[:, None, :], (Z, SHARE, TOK)).reshape(TILE, TOK)
        lane = lax.broadcasted_iota(jnp.int32, (TILE, TOK), 1)
        flag = jnp.sum(jnp.where(lane == khalf * HALF + offset, wide, 0.0), axis=1, keepdims=True)
        last = jnp.where(flag > 0.5, pos + DELAY - 1, BLOCKS * HALF)
        krow = pl.multiple_of(khalf * SHARE, SHARE)
        vrow = pl.multiple_of((2 + khalf) * SHARE, SHARE)
        k = kmsg_ref[:, pl.ds(krow, SHARE), :].reshape(TILE, HEAD)
        v = kmsg_ref[:, pl.ds(vrow, SHARE), :].reshape(TILE, HEAD)
        return k, v, pos, last

    def stat_row(self, qmsg_ref, qhalf, which):
        rows = []
        for peer in range(X):
            both = qmsg_ref[peer, STAT : STAT + 16, :].astype(F32)

            def total(b):
                at = b * 6 + which * 3
                return both[at : at + 1] + both[at + 1 : at + 2] + both[at + 2 : at + 3]

            rows.append(jnp.where(qhalf == 0, total(0), total(1)))
        return jnp.concatenate(rows, axis=1)

    def pair(self, qhalf, khalf, slots=(0, 1)):
        q0 = pl.multiple_of(qhalf * TOK, TOK)
        d0 = pl.multiple_of((2 + qhalf) * TOK, TOK)
        norm = self.stat_row(self.qmsg_ref, qhalf, 0)
        delta = self.stat_row(self.qmsg_ref, qhalf, 1)
        qblock = jnp.where(qhalf == 0, CORE * self.chip + self.core, BLOCKS - 1 - CORE * self.chip - self.core)
        qpos = qblock * HALF + lax.broadcasted_iota(jnp.int32, (1, QSLOT), 1) % HALF
        q = self.qmsg_ref[:, pl.ds(q0, TOK), :].reshape(QSLOT, HEAD)
        do = self.qmsg_ref[:, pl.ds(d0, TOK), :].reshape(QSLOT, HEAD)
        for slot in slots:
            k, v, kpos, klast = self.keys(slot, khalf)
            s = lax.dot_general(k, q, (((1,), (1,)), ((), ())), preferred_element_type=F32)
            dp = lax.dot_general(v, do, (((1,), (1,)), ((), ())), preferred_element_type=F32)
            seen = qpos <= klast
            if not self.other:
                seen &= kpos <= qpos
            w = jnp.where(seen, jnp.exp2(s * (SCALE * LOG2E) - norm), 0.0)
            ds = ((w * SCALE) * (dp - delta)).astype(BF16)
            wb = w.astype(BF16)
            self.dv_acc[slot, khalf] += jnp.dot(wb, do, preferred_element_type=F32)
            self.dk_acc[slot, khalf] += jnp.dot(ds, q, preferred_element_type=F32)
            self.dq_acc[qhalf] += lax.dot_general(ds, k, (((0,), (0,)), ((), ())), preferred_element_type=F32)

    def write_keys(self, slot, out_ref):
        for khalf in range(2):
            dk = self.dk_acc[slot, khalf].reshape(Z, SHARE, HEAD)
            dv = self.dv_acc[slot, khalf].reshape(Z, SHARE, HEAD)
            out_ref[:, khalf * SHARE : (khalf + 1) * SHARE, :] = dk
            out_ref[:, (2 + khalf) * SHARE : (3 + khalf) * SHARE, :] = dv

    def write_queries(self, out_ref):
        for peer in range(X):
            for b in range(2):
                for h in range(2):
                    r = peer * TOK + h * HALF
                    value = self.dq_acc[b, r : r + HALF, :]
                    out_ref[peer, b * HALF : (b + 1) * HALF, h * HEAD : (h + 1) * HEAD] = value


OWN_PAIRS = ((0, 0), (1, 0), (1, 1))


def own_first_kernel(kown_ref, qown_ref, dk_out, dv_out, dq_out):
    grads = Grads((kown_ref,), qown_ref, False, dk_out, dv_out, dq_out)
    dk_out[...] = jnp.zeros_like(dk_out)
    dv_out[...] = jnp.zeros_like(dv_out)
    dq_out[...] = jnp.zeros_like(dq_out)
    for qhalf, khalf in OWN_PAIRS:
        grads.pair(qhalf, khalf, (0,))


def own_second_kernel(kpeer_ref, qown_ref, dq_ref, dk_out, dv_out, dq_out, dq_acc):
    grads = Grads((None, kpeer_ref), qown_ref, False, {}, {}, dq_acc)
    dk_out[...] = jnp.zeros_like(dk_out)
    dv_out[...] = jnp.zeros_like(dv_out)
    dq_acc[...] = dq_ref[...]
    grads.dk_acc, grads.dv_acc = Shifted(dk_out), Shifted(dv_out)
    for qhalf, khalf in OWN_PAIRS:
        grads.pair(qhalf, khalf, (1,))
    grads.write_queries(dq_out)


class Shifted:
    def __init__(self, ref):
        self.ref = ref

    def __getitem__(self, index):
        return self.ref[index[0] - 1, index[1]]

    def __setitem__(self, index, value):
        self.ref[index[0] - 1, index[1]] = value


def other_kernel(
    kown_ref,
    kpeer_ref,
    qother_ref,
    dk0_ref,
    dv0_ref,
    dk1_ref,
    dv1_ref,
    mine_out,
    theirs_out,
    dq_out,
    dk_acc,
    dv_acc,
    dq_acc,
):
    grads = Grads((kown_ref, kpeer_ref), qother_ref, True, dk_acc, dv_acc, dq_acc)
    dk_acc[0] = dk0_ref[0]
    dk_acc[1] = dk1_ref[0]
    dv_acc[0] = dv0_ref[0]
    dv_acc[1] = dv1_ref[0]
    dq_acc[...] = jnp.zeros_like(dq_acc)
    column = lax.axis_index("yl")
    for qhalf, khalf in ((1, 0), (column, column)):
        grads.pair(qhalf, khalf)
    grads.write_keys(0, mine_out)
    grads.write_keys(1, theirs_out)
    grads.write_queries(dq_out)


def merge_kernel(own_ref, got_ref, out_ref):
    out_ref[...] = (own_ref[...] + got_ref[...]).astype(BF16)


def dq_add_kernel(keep_ref, got_ref, *out_refs):
    part = lax.axis_index("x")
    for shift in range(X):
        to = (part + shift) % X
        out_refs[shift][...] = keep_ref[to] + got_ref[to]


def dq_sum_kernel(*refs):
    *in_refs, out_ref = refs
    total = in_refs[0][...]
    for ref in in_refs[1:]:
        total += ref[...]
    out_ref[...] = total.astype(BF16)


def dkv_sum_kernel(in_ref, out_ref):
    total = in_ref[0].astype(F32)
    for peer in range(1, Z):
        total += in_ref[peer].astype(F32)
    rows = total.astype(BF16)
    for peer in range(YH * X):
        out_ref[peer] = rows


def unpack_kernel(in_ref, dk_ref, dv_ref):
    for g in range(YH):
        for x in range(X):
            for b in range(2):
                at = b * HALF + x * SHARE
                dk_ref[g, at : at + SHARE, :] = in_ref[g * X + x, b * SHARE : (b + 1) * SHARE, :]
                dv_ref[g, at : at + SHARE, :] = in_ref[g * X + x, (2 + b) * SHARE : (3 + b) * SHARE, :]


def call(kernel, outs, n_in, scratch=(), flops=0, moved=1 << 20, vmem=8):
    shapes = tuple(jax.ShapeDtypeStruct(s, d) for s, d in outs)
    single = len(shapes) == 1
    return pl.pallas_call(
        kernel,
        out_shape=shapes[0] if single else shapes,
        in_specs=[VMEM_SPEC] * n_in,
        out_specs=VMEM_SPEC if single else (VMEM_SPEC,) * len(shapes),
        scratch_shapes=list(scratch),
        compiler_params=pltpu.CompilerParams(vmem_limit_bytes=vmem << 20),
        cost_estimate=pl.CostEstimate(flops=flops, bytes_accessed=moved, transcendentals=0),
    )


def exchange(value, axes):
    return lax.all_to_all(value, axes, 0, 0, tiled=True)


def shifted(value, axis, size, shift):
    return lax.ppermute(value, axis, [(i, (i + shift) % size) for i in range(size)])


def local(queries, key_codes, key_scale, value_codes, value_scale, evict_flags, out_forward, grad_output, log_norm):
    kmsg, qmsg = call(prep_kernel, [((Z, KMSG, HEAD), BF16), ((QMSG, HEAD), BF16)], 9, vmem=56)(
        key_codes,
        key_scale,
        value_codes,
        value_scale,
        evict_flags,
        queries,
        grad_output,
        out_forward,
        log_norm,
    )
    kown = exchange(kmsg, "z")
    qmine = lax.all_gather(qmsg, "x", axis=0)
    qother = shifted(qmine, "yl", YL, 1)
    kpeer = shifted(kown, "core", CORE, 1)
    work = 5 * 2 * TILE * QHALF * HEAD
    acc = ((CORE, 2, TILE, HEAD), F32)
    half_acc = ((1, 2, TILE, HEAD), F32)
    dq_acc = ((2, QSLOT, HEAD), F32)
    dkv_shape = ((Z, KROWS, HEAD), F32)
    piece = ((X, TOK, 2 * HEAD), F32)
    dk0, dv0, dq = call(own_first_kernel, [half_acc, half_acc, dq_acc], 2, flops=work * 3 // 2, vmem=24)(kown, qmine)
    dk1, dv1, keep = call(
        own_second_kernel, [half_acc, half_acc, piece], 3, scratch=[pltpu.VMEM(*dq_acc)], flops=work * 3 // 2, vmem=24
    )(kpeer, qmine, dq)
    mine, theirs, send = call(
        other_kernel,
        [dkv_shape, dkv_shape, piece],
        7,
        scratch=[pltpu.VMEM(*acc), pltpu.VMEM(*acc), pltpu.VMEM(*dq_acc)],
        flops=2 * work,
        vmem=24,
    )(kown, kpeer, qother, dk0, dv0, dk1, dv1)
    dkv_got = shifted(theirs, "core", CORE, 1)
    got = shifted(send, "yl", YL, 1)
    dkv = call(merge_kernel, [((Z, KROWS, HEAD), BF16)], 2)(mine, dkv_got)
    dkv = exchange(dkv, "z")
    parts = call(dq_add_kernel, [((TOK, 2 * HEAD), F32)] * X, 2)(keep, got)
    home = [parts[0]]
    for k in range(1, X):
        home.append(shifted(parts[k], "x", X, k))
    grad_queries = call(dq_sum_kernel, [((TOK, 2 * HEAD), BF16)], X)(*home)
    final = call(dkv_sum_kernel, [((YH * X, KROWS, HEAD), BF16)], 1)(dkv)
    every = exchange(final, ("yh", "x"))
    grad_keys, grad_values = call(unpack_kernel, [((2, TOK, HEAD), BF16)] * 2, 1)(every)
    return grad_queries, grad_keys, grad_values


def solution(mesh):
    fine = Mesh(mesh.devices.reshape(YL, Z, CORE, YH, X), ("yl", "z", "core", "yh", "x"))
    ctx, head = ("yl", "z", "core"), ("yh", "x")
    in_specs = (
        P(ctx, head),
        P(None, ctx, None),
        P(None, ctx),
        P(None, ctx, None),
        P(None, ctx),
        P(None, ctx),
        P(ctx, head),
        P(ctx, head),
        P(head, ctx),
    )
    out_specs = (P(ctx, head), P(None, ctx, None), P(None, ctx, None))
    return jax.shard_map(local, mesh=fine, in_specs=in_specs, out_specs=out_specs, check_vma=False)
```
